32 devices in a mesh: tok: 8 (over z, x), head: 4 (over y, core).
Axes of the slice: x: 2, y: 2, z: 4, core: 2. Of those that a mesh axis runs over, the one named last changes fastest.
Arguments:
- tri_tokens: bfloat16 [4096, 1024], P(('tok', 'head')), may hold values from -6 to 6
- image_tokens: bfloat16 [32768, 1024], P('tok'), may hold values from -6 to 6
- cross_q: bfloat16 [1024, 1024], P(None, 'head'), may hold values from -0.1875 to 0.1875
- cross_kv: bfloat16 [2, 1024, 1024], P(None, None, 'head'), may hold values from -0.1875 to 0.1875
- cross_out: bfloat16 [1024, 1024], P('head'), may hold values from -0.1875 to 0.1875
- self_qkv: bfloat16 [3, 1024, 1024], P(None, None, 'head'), may hold values from -0.1875 to 0.1875
- self_out: bfloat16 [1024, 1024], P('head'), may hold values from -0.1875 to 0.1875
- mlp_in: bfloat16 [1024, 4096], P(None, 'head'), may hold values from -0.1875 to 0.1875
- mlp_out: bfloat16 [4096, 1024], P('head'), may hold values from -0.09375 to 0.09375
Outputs:
- tri_out: bfloat16 [4096, 1024], P(('tok', 'head'))
The draws below stay inside these ranges and needn't reach their ends.
All inputs are finite; a program needn't handle non-finite values.
Results may differ from the reference program's by a relative error of at most 0.013.
Values may be sent and summed in bfloat16 or wider, within the bound.
A program may use at most 128 MiB of HBM per device.

```python
import math
import jax
import jax.numpy as jnp
from jax import lax

D = 1024
HEADS = 16
FF = 4096
TRI = 4096
IMG = 32768


def level_of(key, extent, cuts, least, top_value):
    factor_of = 1.0
    for axis_at, blocks in cuts:
        steps = jax.random.uniform(jax.random.fold_in(jax.random.fold_in(key, 6), axis_at), (blocks,), jnp.float32, least / len(cuts), top_value / len(cuts))
        factor_of = factor_of * jnp.repeat(jnp.exp(steps), extent[axis_at] // blocks).reshape((-1,) + (1,) * (len(extent) - 1 - axis_at))
    return factor_of


def scatter_about(rng, extent, deviation, reach, pieces=(), dtype=jnp.bfloat16):
    values = jax.random.normal(rng, extent, jnp.float32) * deviation
    if len(pieces) > 0:
        values = level_of(rng, extent, pieces, -0.22, 0.18) * values
    return jnp.clip(values, min=-reach, max=reach).astype(dtype)


def setup_inputs(seed: int = 0) -> dict:
    key_of = jax.random.split(jax.random.key(seed), 10)
    return {
        "tri_tokens": scatter_about(key_of[0], (TRI, D), 1.0, 6.0, ((0, 32),)),
        "image_tokens": scatter_about(key_of[1], (IMG, D), 1.0, 6.0, ((0, 8),)),
        "cross_q": scatter_about(key_of[2], (D, D), D ** -0.5, 0.1875, ((1, 4),)),
        "cross_kv": scatter_about(key_of[3], (2, D, D), D ** -0.5, 0.1875, ((2, 4),)),
        "cross_out": scatter_about(key_of[4], (D, D), D ** -0.5, 0.1875, ((0, 4),)),
        "self_qkv": scatter_about(key_of[5], (3, D, D), D ** -0.5, 0.1875, ((2, 4),)),
        "self_out": scatter_about(key_of[6], (D, D), D ** -0.5, 0.1875, ((0, 4),)),
        "mlp_in": scatter_about(key_of[7], (D, FF), D ** -0.5, 0.1875, ((1, 4),)),
        "mlp_out": scatter_about(key_of[8], (FF, D), FF ** -0.5, 0.09375, ((0, 4),)),
    }


score_gain = 2.5

def layer_norm(values):
    centered = values - lax.optimization_barrier(jnp.mean(values, axis=-1, keepdims=True))
    return centered * lax.rsqrt(lax.optimization_barrier(jnp.mean(centered * centered, axis=-1, keepdims=True)) + 1e-05)

def head_norm(values, head_count):
    shaped = values.reshape(values.shape[0], head_count, -1)
    normed = shaped * lax.rsqrt(lax.optimization_barrier(jnp.mean(shaped * shaped, axis=-1, keepdims=True)) + 1e-06)
    return normed.reshape(values.shape[0], -1).astype(jnp.bfloat16)

def partial_attention(queries, kv_rows, head_count):
    query_count = queries.shape[0]
    head_size = queries.shape[1] // head_count
    score_scale = score_gain / math.sqrt(head_size)
    query_block = math.gcd(query_count, 512)
    key_block = math.gcd(kv_rows.shape[0], 2048)
    query_blocks = queries.reshape(query_count // query_block, query_block, head_count, head_size)
    key_blocks = kv_rows.reshape(kv_rows.shape[0] // key_block, key_block, 2, head_count, head_size)

    def one_block(query_tile):

        def key_step(running, key_tile):
            weighted, totals = running
            scores = jnp.einsum('qhd,khd->qhk', query_tile, key_tile[:, 0], preferred_element_type=jnp.float32) * score_scale
            exp_scores = jnp.exp(scores)
            totals = totals + lax.optimization_barrier(jnp.sum(exp_scores, axis=-1))
            weighted = weighted + jnp.einsum('qhk,khd->qhd', exp_scores.astype(jnp.bfloat16), key_tile[:, 1], preferred_element_type=jnp.float32)
            return ((weighted, totals), None)
        starting = (jnp.zeros((query_block, head_count, head_size), jnp.float32), jnp.zeros((query_block, head_count), jnp.float32))
        result, _ = lax.scan(key_step, starting, key_blocks)
        return result
    weighted, totals = lax.map(one_block, query_blocks)
    return (weighted.reshape(query_count, head_count, head_size), totals.reshape(query_count, head_count))

def finish(weighted, totals):
    return (weighted / totals[:, :, None]).reshape(weighted.shape[0], -1).astype(jnp.bfloat16)

def reference(tri_tokens, image_tokens, cross_q, cross_kv, cross_out, self_qkv, self_out, mlp_in, mlp_out):
    stream_zero = tri_tokens.astype(jnp.float32)
    normed_one = layer_norm(stream_zero).astype(jnp.bfloat16)
    queries = head_norm(jnp.dot(normed_one, cross_q, preferred_element_type=jnp.float32), HEADS)
    kv_weight = jnp.concatenate([cross_kv[0], cross_kv[1]], axis=1)
    image_kv = jnp.dot(image_tokens, kv_weight, preferred_element_type=jnp.float32)
    view_kv = jnp.concatenate([head_norm(image_kv[:, :D], HEADS), image_kv[:, D:].astype(jnp.bfloat16)], axis=1)
    weighted, totals = partial_attention(queries, view_kv, HEADS)
    cross_mix = finish(weighted, totals)
    stream_one = stream_zero + jnp.dot(cross_mix, cross_out, preferred_element_type=jnp.float32)
    normed_two = layer_norm(stream_one).astype(jnp.bfloat16)
    self_weight = jnp.concatenate([self_qkv[0], self_qkv[1], self_qkv[2]], axis=1)
    mixed = jnp.dot(normed_two, self_weight, preferred_element_type=jnp.float32)
    self_queries = head_norm(mixed[:, :D], HEADS)
    self_kv = jnp.concatenate([head_norm(mixed[:, D:2 * D], HEADS), mixed[:, 2 * D:].astype(jnp.bfloat16)], axis=1)
    weighted, totals = partial_attention(self_queries, self_kv, HEADS)
    self_mix = finish(weighted, totals)
    stream_two = stream_one + jnp.dot(self_mix, self_out, preferred_element_type=jnp.float32)
    normed_three = layer_norm(stream_two).astype(jnp.bfloat16)
    hidden = jax.nn.gelu(jnp.dot(normed_three, mlp_in, preferred_element_type=jnp.float32), approximate=True).astype(jnp.bfloat16)
    return (stream_two + jnp.dot(hidden, mlp_out, preferred_element_type=jnp.float32)).astype(jnp.bfloat16)
```

```python
import functools
import math

import jax
import jax.numpy as jnp
from jax import lax
from jax.experimental import pallas as pl
from jax.experimental.pallas import tpu as pltpu
from jax.sharding import PartitionSpec as P

HEADS = 16
score_gain = 2.5
VMEM_LIMIT = 60 << 20
MESH = pl.DeviceIdType.MESH
ONES = 16
bf16 = jnp.bfloat16
f32 = jnp.float32


def layer_norm(values):
    centered = values - jnp.mean(values, axis=-1, keepdims=True)
    return centered * lax.rsqrt(jnp.mean(centered * centered, axis=-1, keepdims=True) + 1e-05)


def dot(a, b):
    return jnp.dot(a, b, preferred_element_type=f32)


def head_scale(product, head_size):
    width = product.shape[1]
    rows = lax.broadcasted_iota(jnp.int32, (width, width), 0) // head_size
    cols = lax.broadcasted_iota(jnp.int32, (width, width), 1) // head_size
    same = (rows == cols).astype(f32).astype(bf16)
    squares = product * product
    high = squares.astype(bf16)
    low = (squares - high.astype(f32)).astype(bf16)
    total = dot(high, same) + dot(low, same)
    return lax.rsqrt(total * (1.0 / head_size) + 1e-06)


def head_norm_rows(product, head_size, factor):
    width, count = product.shape
    shaped = product.reshape(width // head_size, head_size, count)
    mean = jnp.sum(shaped * shaped, axis=1, keepdims=True) * (1.0 / head_size)
    return (shaped * (lax.rsqrt(mean + 1e-06) * factor)).reshape(width, count)


def send(source, target, send_sem, recv_sem, device):
    copy = pltpu.make_async_remote_copy(
        src_ref=source,
        dst_ref=target,
        send_sem=send_sem,
        recv_sem=recv_sem,
        device_id=device,
        device_id_type=MESH,
    )
    return copy


def greet(devices):
    barrier = pltpu.get_barrier_semaphore()
    for device in devices:
        pl.semaphore_signal(barrier, inc=1, device_id=device, device_id_type=MESH)
    pl.semaphore_wait(barrier, len(devices))


class Place:
    def __init__(self, toks, heads):
        self.toks, self.heads = toks, heads
        self.tok, self.head = lax.axis_index("tok"), lax.axis_index("head")
        self.pairs = heads // 2
        self.pair, self.core = lax.div(self.head, 2), lax.rem(self.head, 2)

    def partner(self):
        return (self.tok, self.pair * 2 + 1 - self.core)

    def pair_at(self, k):
        return lax.rem(self.pair + k + self.pairs, self.pairs)

    def across(self, k):
        return (self.tok, self.pair_at(k) * 2 + self.core)

    def head_peers(self):
        return [self.partner()] + [self.across(k) for k in range(1, self.pairs)]


class Gather:
    @staticmethod
    def scratch(heads, rows, depth):
        dma = pltpu.SemaphoreType.DMA((heads // 2,))
        return [pltpu.VMEM((heads, rows, depth), bf16), dma, dma, dma, dma]

    def __init__(self, place, refs):
        self.place = place
        self.rows, self.pair_out, self.pair_in, self.far_out, self.far_in = refs

    def far(self, k):
        p = self.place
        mine = self.rows.at[p.head]
        return send(mine, mine, self.far_out.at[k], self.far_in.at[k], p.across(k))

    def far_arrival(self, k):
        p = self.place
        slot = self.rows.at[p.pair_at(-k) * 2 + p.core]
        return send(slot, slot, self.far_out.at[k], self.far_in.at[k], p.across(-k))

    def near(self, k):
        p = self.place
        slot = self.rows.at[p.pair_at(-k) * 2 + p.core]
        return send(slot, slot, self.pair_out.at[k], self.pair_in.at[k], p.partner())

    def near_arrival(self, k):
        p = self.place
        slot = self.rows.at[p.pair_at(-k) * 2 + 1 - p.core]
        return send(slot, slot, self.pair_out.at[k], self.pair_in.at[k], p.partner())

    def start(self, value):
        self.rows[self.place.head] = value
        for k in range(1, self.place.pairs):
            self.far(k).start()
        self.near(0).start()

    def forward(self):
        for k in range(1, self.place.pairs):
            self.far_arrival(k).wait_recv()
            self.near(k).start()

    def finish(self):
        for k in range(self.place.pairs):
            self.near_arrival(k).wait_recv()

    def drain(self):
        for k in range(1, self.place.pairs):
            self.far(k).wait_send()
        for k in range(self.place.pairs):
            self.near(k).wait_send()


def join(tiles, width):
    total = functools.reduce(lambda a, b: a + b, [t.astype(f32) for t in tiles])
    return total[:width], total[width : width + 8] + total[width + 8 : width + 16]


def pack(mixed, totals):
    high = totals.astype(bf16).astype(f32)
    return jnp.concatenate([mixed, high, totals - high], axis=0).astype(bf16)


def attend_block(queries, k_ref, vt_ref, head_size):
    width, count = queries.shape
    lanes = min(128, width)
    keys = k_ref.shape[0]
    block = math.gcd(keys, 2048)
    row = lax.broadcasted_iota(jnp.int32, (lanes, count), 0) // head_size
    place = lax.broadcasted_iota(jnp.int32, (ONES, count), 0) % 8
    mixed, totals = [], jnp.zeros((ONES, count), f32)
    for h in range(width // head_size):
        first = h * head_size // lanes * lanes
        picked = queries[first : first + lanes]
        if lanes > head_size:
            picked = jnp.where(row == h % (lanes // head_size), picked, jnp.zeros_like(picked))
        acc = jnp.zeros((head_size + ONES, count), f32)
        for i in range(keys // block):
            rows = slice(i * block, (i + 1) * block)
            scores = dot(k_ref[rows, first : first + lanes], picked)
            acc = acc + dot(vt_ref[h, :, rows], jnp.exp2(scores).astype(bf16))
        mixed.append(acc[:head_size])
        totals = jnp.where(place == h, acc[head_size:], totals)
    return pack(jnp.concatenate(mixed, axis=0), totals[:8])


def cross_kernel(
    tri_ref, image_ref, wq_ref, wkv_ref, out_ref,
    image, k_ref, vt_ref, queries, tiles, pair_tiles, joined, far_tiles,
    image_sem, q_out, q_in, f_out, f_in, p_out, p_in, c_out, c_in, *gather_refs,
    toks, heads, head_size, factor,
):
    place = Place(toks, heads)
    width, group = out_ref.shape
    lines = toks // 2
    line, side = lax.div(place.tok, 2), lax.rem(place.tok, 2)
    neighbour = (line * 2 + 1 - side, place.head)

    def line_at(k):
        return lax.rem(line + k + lines, lines)

    def peer(k):
        return (line_at(k) * 2 + side, place.head)

    keys = k_ref.shape[0]
    step_rows = math.gcd(keys, 512)
    steps = keys // step_rows

    def fetch(i):
        rows = pl.ds(pl.multiple_of(i * step_rows, step_rows), step_rows)
        return pltpu.make_async_copy(image_ref.at[rows], image.at[rows], image_sem.at[i])

    for i in range(steps):
        fetch(i).start()
    greet(place.head_peers() + [neighbour] + [peer(k) for k in range(1, lines)])
    gather = Gather(place, gather_refs)
    gather.start(layer_norm(tri_ref[...].astype(f32)).astype(bf16))
    vt_ref[:, head_size:, :] = jnp.ones((width // head_size, ONES, keys), bf16)

    def q_send(k):
        mine = queries.at[place.tok]
        return send(mine, mine, q_out.at[k], q_in.at[k], peer(-k) if k else neighbour)

    def q_arrival(k):
        slot = queries.at[line_at(k) * 2 + side]
        return send(slot, slot, q_out.at[k], q_in.at[k], peer(k))

    def project(i, carry):
        @pl.when(i == steps // 2)
        def _():
            gather.forward()

        @pl.when(i == steps * 3 // 4)
        def _():
            gather.finish()
            x = gather.rows[...].reshape(group, -1)
            product = jnp.transpose(dot(x, wq_ref[...]))
            queries[place.tok] = head_norm_rows(product, head_size, factor).astype(bf16)
            if lines > 1:
                q_send(1).start()

        rows = pl.ds(pl.multiple_of(i * step_rows, step_rows), step_rows)
        fetch(i).wait()
        x = image[rows, :]
        k = dot(x, wkv_ref[0])
        k_ref[rows, :] = (k * head_scale(k, head_size)).astype(bf16)
        v = jnp.transpose(dot(x, wkv_ref[1])).astype(bf16)
        vt_ref[:, :head_size, rows] = v.reshape(width // head_size, head_size, step_rows)
        return carry

    lax.fori_loop(0, steps, project, 0)
    for k in range(2, lines):
        q_send(k).start()
    q_send(0).start()

    def forward(k, slot):
        block = queries.at[slot]
        return send(block, block, f_out.at[k], f_in.at[k], neighbour)

    def pair_send(k, s):
        return send(tiles.at[s], pair_tiles.at[k], p_out.at[k], p_in.at[k], neighbour)

    def far_send(k):
        return send(joined.at[k], far_tiles.at[k], c_out.at[k], c_in.at[k], peer(k))

    def attend(s, carry):
        k = lax.div(s, 2) + 1
        last = k == lines
        first = lax.rem(s, 2) == 0
        mine = first != last
        slot = lax.rem(line + k, lines) * 2 + jnp.where(mine, side, 1 - side)

        @pl.when(jnp.logical_and(first, jnp.logical_not(last)))
        def _():
            block = queries.at[slot]
            send(block, block, q_out.at[k], q_in.at[k], neighbour).wait_recv()
            forward(k, slot).start()

        @pl.when(jnp.logical_and(jnp.logical_not(first), jnp.logical_not(last)))
        def _():
            forward(k, slot).wait_recv()

        @pl.when(jnp.logical_and(first, last))
        def _():
            block = queries.at[slot]
            send(block, block, q_out.at[0], q_in.at[0], neighbour).wait_recv()

        tiles[s] = attend_block(queries[slot], k_ref, vt_ref, head_size)

        @pl.when(jnp.logical_not(mine))
        def _():
            pair_send(k, s).start()

        @pl.when(jnp.logical_and(first, k > 1))
        def _():
            before = k - 1
            pair_send(before, s).wait_recv()
            joined[before] = pack(*join([tiles[2 * before - 2], pair_tiles[before]], width))
            far_send(before).start()

        return carry

    lax.fori_loop(0, 2 * lines, attend, 0)
    pair_send(lines, 0).wait_recv()
    for k in range(1, lines):
        far_send(k).wait_recv()
    mixed, totals = join(
        [tiles[2 * lines - 1], pair_tiles[lines]] + [far_tiles[k] for k in range(1, lines)], width
    )
    for h in range(width // head_size):
        rows = slice(h * head_size, (h + 1) * head_size)
        out_ref[rows, :] = (mixed[rows] / totals[h : h + 1]).astype(bf16)
    gather.drain()
    for k in range(lines):
        q_send(k).wait_send()
    for k in range(1, lines):
        forward(k, 0).wait_send()
        far_send(k).wait_send()
    for k in range(1, lines + 1):
        pair_send(k, 0).wait_send()


def cross(tri, image, wq, wkv, toks, heads, head_size, factor):
    rows, depth = tri.shape
    keys = image.shape[0]
    width = wq.shape[1]
    group = rows * heads
    lines = toks // 2
    tile = (width + 16, group)
    vmem = pl.BlockSpec(memory_space=pltpu.VMEM)
    dma = pltpu.SemaphoreType.DMA
    return pl.pallas_call(
        functools.partial(
            cross_kernel, toks=toks, heads=heads, head_size=head_size, factor=factor
        ),
        out_shape=jax.ShapeDtypeStruct((width, group), bf16),
        in_specs=[vmem, pl.BlockSpec(memory_space=pl.ANY), vmem, vmem],
        out_specs=vmem,
        scratch_shapes=[
            pltpu.VMEM((keys, depth), bf16),
            pltpu.VMEM((keys, width), bf16),
            pltpu.VMEM((width // head_size, head_size + ONES, keys), bf16),
            pltpu.VMEM((toks, width, group), bf16),
            pltpu.VMEM((2 * lines,) + tile, bf16),
            pltpu.VMEM((lines + 1,) + tile, bf16),
            pltpu.VMEM((lines,) + tile, bf16),
            pltpu.VMEM((lines,) + tile, bf16),
            dma((keys // math.gcd(keys, 512),)),
            dma((lines,)), dma((lines,)),
            dma((lines,)), dma((lines,)),
            dma((lines + 1,)), dma((lines + 1,)),
            dma((lines,)), dma((lines,)),
        ] + Gather.scratch(heads, rows, depth),
        compiler_params=pltpu.CompilerParams(
            vmem_limit_bytes=VMEM_LIMIT, collective_id=0, has_side_effects=True
        ),
        name="cross",
    )(tri, image, wq, wkv)


def project_kernel(x_ref, w_ref, *out_refs, plan, head_size):
    width = w_ref.shape[2]
    for j, (place, column, factor) in enumerate(plan):
        product = jnp.dot(x_ref[...], w_ref[j], preferred_element_type=jnp.float32)
        if factor is not None:
            product = product * (head_scale(product, head_size) * factor)
        out_refs[place][:, column * width : (column + 1) * width] = product.astype(jnp.bfloat16)


def project(x, weights, plan, head_size):
    rows, depth = x.shape
    count, _, width = weights.shape
    block = math.gcd(rows, 512)
    places = max(p for p, _, _ in plan) + 1
    widths = [width * sum(p == place for p, _, _ in plan) for place in range(places)]
    return pl.pallas_call(
        functools.partial(project_kernel, plan=plan, head_size=head_size),
        out_shape=[jax.ShapeDtypeStruct((rows, w), jnp.bfloat16) for w in widths],
        grid=(rows // block,),
        in_specs=[
            pl.BlockSpec((block, depth), lambda i: (i, 0)),
            pl.BlockSpec((count, depth, width), lambda i: (0, 0, 0)),
        ],
        out_specs=[pl.BlockSpec((block, w), lambda i: (i, 0)) for w in widths],
        compiler_params=pltpu.CompilerParams(vmem_limit_bytes=VMEM_LIMIT),
        cost_estimate=pl.CostEstimate(
            flops=2 * rows * depth * width * count,
            bytes_accessed=2 * (rows * depth + count * depth * width + rows * width * count),
            transcendentals=rows * width,
        ),
    )(x, weights)


def stack_heads(queries, head_size):
    rows, lanes = queries.shape
    lane = lax.broadcasted_iota(jnp.int32, (rows, lanes), 1) // head_size
    zero = jnp.zeros_like(queries)
    heads = lanes // head_size
    if heads == 1:
        return queries
    return jnp.concatenate([jnp.where(lane == h, queries, zero) for h in range(heads)], axis=0)


def pick_heads(acc_ref, rows, lanes, head_size):
    picked = acc_ref[:rows, :]
    lane = lax.broadcasted_iota(jnp.int32, picked.shape, 1) % lanes // head_size
    for h in range(1, lanes // head_size):
        picked = jnp.where(lane == h, acc_ref[h * rows : (h + 1) * rows, :], picked)
    return picked[:, :lanes], picked[:, lanes:]


def fold_keys(stacked, key_of, value_of, acc_ref, key_count, lanes):
    block = math.gcd(key_count, 512)
    ones = jnp.ones((block, lanes), jnp.bfloat16)
    acc_ref[...] = jnp.zeros_like(acc_ref)

    def step(i, carry):
        rows = pl.ds(pl.multiple_of(i * block, block), block)
        scores = lax.dot_general(
            stacked, key_of(rows), (((1,), (1,)), ((), ())), preferred_element_type=jnp.float32
        )
        weights = jnp.exp2(scores).astype(jnp.bfloat16)
        values = jnp.concatenate([value_of(rows), ones], axis=1)
        acc_ref[...] += jnp.dot(weights, values, preferred_element_type=jnp.float32)
        return carry

    lax.fori_loop(0, key_count // block, step, 0, unroll=True)


def attend_kernel(q_ref, k_ref, v_ref, *refs, head_size, finish):
    acc_ref = refs[-1]
    rows, lanes = q_ref.shape
    fold_keys(
        stack_heads(q_ref[...], head_size),
        lambda r: k_ref[r, :],
        lambda r: v_ref[r, :],
        acc_ref,
        k_ref.shape[0],
        lanes,
    )
    mixed, totals = pick_heads(acc_ref, rows, lanes, head_size)
    if finish:
        refs[0][...] = (mixed / totals).astype(jnp.bfloat16)
    else:
        refs[0][...] = mixed.astype(jnp.bfloat16)
        refs[1][...] = totals


def attend(queries, kv, head_size, finish):
    count, width = queries.shape
    keys = kv.shape[0]
    lanes = min(128, width)
    pairs = width // lanes
    block = math.gcd(count, 512)
    outs = [jax.ShapeDtypeStruct((count, width), jnp.bfloat16)]
    if not finish:
        outs.append(jax.ShapeDtypeStruct((count, width), jnp.float32))
    if width % 128:
        keys_values = (kv[:, :width], kv[:, width:])
        shift = 0
    else:
        keys_values = (kv, kv)
        shift = pairs
    result = pl.pallas_call(
        functools.partial(attend_kernel, head_size=head_size, finish=finish),
        out_shape=outs,
        grid=(pairs, count // block),
        in_specs=[
            pl.BlockSpec((block, lanes), lambda p, i: (i, p)),
            pl.BlockSpec((keys, lanes), lambda p, i: (0, p)),
            pl.BlockSpec((keys, lanes), lambda p, i: (0, p + shift)),
        ],
        out_specs=[pl.BlockSpec((block, lanes), lambda p, i: (i, p))] * len(outs),
        scratch_shapes=[pltpu.VMEM((lanes // head_size * block, 2 * lanes), jnp.float32)],
        compiler_params=pltpu.CompilerParams(vmem_limit_bytes=VMEM_LIMIT),
        cost_estimate=pl.CostEstimate(
            flops=16 * count * keys * width,
            bytes_accessed=2 * (3 * count * width + 2 * keys * width),
            transcendentals=count * keys * width // head_size,
        ),
    )(queries, *keys_values)
    return result


def per_device(
    tri_tokens, image_tokens, cross_q, cross_kv, cross_out, self_qkv, self_out, mlp_in, mlp_out,
    *, tok, head
):
    width = cross_q.shape[1]
    head_size = tri_tokens.shape[1] // HEADS
    query_factor = score_gain / math.sqrt(head_size) * math.log2(math.e)

    def spread(stream):
        return lax.all_gather(layer_norm(stream).astype(jnp.bfloat16), "head", axis=0, tiled=True)

    def collect(operand, weight):
        return lax.psum_scatter(
            jnp.dot(operand, weight, preferred_element_type=jnp.float32).astype(jnp.bfloat16),
            "head",
            scatter_dimension=0,
            tiled=True,
        ).astype(jnp.float32)

    stream_zero = tri_tokens.astype(jnp.float32)
    mixed = cross(tri_tokens, image_tokens, cross_q, cross_kv, tok, head, head_size, query_factor)
    mix = mixed.T
    stream_one = stream_zero + collect(mix, cross_out)
    self_queries, self_kv = project(
        spread(stream_one), self_qkv, ((0, 0, query_factor), (1, 0, 1.0), (1, 1, None)), head_size
    )
    all_kv = lax.all_gather(self_kv, "tok", axis=0, tiled=True)
    (mix,) = attend(self_queries, all_kv, head_size, True)
    stream_two = stream_one + collect(mix, self_out)
    hidden = jax.nn.gelu(
        jnp.dot(spread(stream_two), mlp_in, preferred_element_type=jnp.float32), approximate=True
    ).astype(jnp.bfloat16)
    return (stream_two + collect(hidden, mlp_out)).astype(jnp.bfloat16)


def solution(mesh):
    return jax.shard_map(
        functools.partial(per_device, tok=mesh.shape["tok"], head=mesh.shape["head"]),
        mesh=mesh,
        in_specs=(
            P(("tok", "head"), None),
            P("tok", None),
            P(None, "head"),
            P(None, None, "head"),
            P("head", None),
            P(None, None, "head"),
            P("head", None),
            P(None, "head"),
            P("head", None),
        ),
        out_specs=P(("tok", "head"), None),
        check_vma=False,
    )
```

```python
import functools
import math

import jax
import jax.numpy as jnp
from jax import lax
from jax.experimental import pallas as pl
from jax.experimental.pallas import tpu as pltpu
from jax.sharding import PartitionSpec as P

HEADS = 16
score_gain = 2.5
VMEM_LIMIT = 60 << 20
MESH = pl.DeviceIdType.MESH
ONES = 16
bf16 = jnp.bfloat16
f32 = jnp.float32


def layer_norm(values):
    centered = values - jnp.mean(values, axis=-1, keepdims=True)
    return centered * lax.rsqrt(jnp.mean(centered * centered, axis=-1, keepdims=True) + 1e-05)


def dot(a, b):
    return jnp.dot(a, b, preferred_element_type=f32)


def head_scale(product, head_size):
    width = product.shape[1]
    rows = lax.broadcasted_iota(jnp.int32, (width, width), 0) // head_size
    cols = lax.broadcasted_iota(jnp.int32, (width, width), 1) // head_size
    same = (rows == cols).astype(f32).astype(bf16)
    squares = product * product
    high = squares.astype(bf16)
    low = (squares - high.astype(f32)).astype(bf16)
    total = dot(high, same) + dot(low, same)
    return lax.rsqrt(total * (1.0 / head_size) + 1e-06)


def head_norm_rows(product, head_size, factor):
    width, count = product.shape
    shaped = product.reshape(width // head_size, head_size, count)
    mean = jnp.sum(shaped * shaped, axis=1, keepdims=True) * (1.0 / head_size)
    return (shaped * (lax.rsqrt(mean + 1e-06) * factor)).reshape(width, count)


def send(source, target, send_sem, recv_sem, device):
    copy = pltpu.make_async_remote_copy(
        src_ref=source,
        dst_ref=target,
        send_sem=send_sem,
        recv_sem=recv_sem,
        device_id=device,
        device_id_type=MESH,
    )
    return copy


def greet(devices):
    barrier = pltpu.get_barrier_semaphore()
    for device in devices:
        pl.semaphore_signal(barrier, inc=1, device_id=device, device_id_type=MESH)
    pl.semaphore_wait(barrier, len(devices))


class Place:
    def __init__(self, toks, heads):
        self.toks, self.heads = toks, heads
        self.tok, self.head = lax.axis_index("tok"), lax.axis_index("head")
        self.pairs = heads // 2
        self.pair, self.core = lax.div(self.head, 2), lax.rem(self.head, 2)

    def partner(self):
        return (self.tok, self.pair * 2 + 1 - self.core)

    def pair_at(self, k):
        return lax.rem(self.pair + k + self.pairs, self.pairs)

    def across(self, k):
        return (self.tok, self.pair_at(k) * 2 + self.core)

    def head_peers(self):
        return [self.partner()] + [self.across(k) for k in range(1, self.pairs)]


class Gather:
    @staticmethod
    def scratch(heads, rows, depth):
        dma = pltpu.SemaphoreType.DMA((heads // 2,))
        return [pltpu.VMEM((heads, rows, depth), bf16), dma, dma, dma, dma]

    def __init__(self, place, refs):
        self.place = place
        self.rows, self.pair_out, self.pair_in, self.far_out, self.far_in = refs

    def far(self, k):
        p = self.place
        mine = self.rows.at[p.head]
        return send(mine, mine, self.far_out.at[k], self.far_in.at[k], p.across(k))

    def far_arrival(self, k):
        p = self.place
        slot = self.rows.at[p.pair_at(-k) * 2 + p.core]
        return send(slot, slot, self.far_out.at[k], self.far_in.at[k], p.across(-k))

    def near(self, k):
        p = self.place
        slot = self.rows.at[p.pair_at(-k) * 2 + p.core]
        return send(slot, slot, self.pair_out.at[k], self.pair_in.at[k], p.partner())

    def near_arrival(self, k):
        p = self.place
        slot = self.rows.at[p.pair_at(-k) * 2 + 1 - p.core]
        return send(slot, slot, self.pair_out.at[k], self.pair_in.at[k], p.partner())

    def start(self, value):
        self.rows[self.place.head] = value
        for k in range(1, self.place.pairs):
            self.far(k).start()
        self.near(0).start()

    def forward(self):
        for k in range(1, self.place.pairs):
            self.far_arrival(k).wait_recv()
            self.near(k).start()

    def finish(self):
        for k in range(self.place.pairs):
            self.near_arrival(k).wait_recv()

    def drain(self):
        for k in range(1, self.place.pairs):
            self.far(k).wait_send()
        for k in range(self.place.pairs):
            self.near(k).wait_send()


def join(tiles, width):
    total = functools.reduce(lambda a, b: a + b, [t.astype(f32) for t in tiles])
    return total[:width], total[width : width + 8] + total[width + 8 : width + 16]


def pack(mixed, totals):
    high = totals.astype(bf16).astype(f32)
    return jnp.concatenate([mixed, high, totals - high], axis=0).astype(bf16)


def attend_block(queries, k_ref, vt_ref, head_size):
    width, count = queries.shape
    lanes = min(128, width)
    keys = k_ref.shape[0]
    block = math.gcd(keys, 2048)
    row = lax.broadcasted_iota(jnp.int32, (lanes, count), 0) // head_size
    place = lax.broadcasted_iota(jnp.int32, (ONES, count), 0) % 8
    mixed, totals = [], jnp.zeros((ONES, count), f32)
    for h in range(width // head_size):
        first = h * head_size // lanes * lanes
        picked = queries[first : first + lanes]
        if lanes > head_size:
            picked = jnp.where(row == h % (lanes // head_size), picked, jnp.zeros_like(picked))
        acc = jnp.zeros((head_size + ONES, count), f32)
        for i in range(keys // block):
            rows = slice(i * block, (i + 1) * block)
            scores = dot(k_ref[rows, first : first + lanes], picked)
            acc = acc + dot(vt_ref[h, :, rows], jnp.exp2(scores).astype(bf16))
        mixed.append(acc[:head_size])
        totals = jnp.where(place == h, acc[head_size:], totals)
    return pack(jnp.concatenate(mixed, axis=0), totals[:8])


def cross_kernel(
    tri_ref, image_ref, wq_ref, wkv_ref, out_ref,
    image, k_ref, vt_ref, queries, tiles, pair_tiles, joined, far_tiles,
    image_sem, q_out, q_in, f_out, f_in, p_out, p_in, c_out, c_in, *gather_refs,
    toks, heads, head_size, factor,
):
    place = Place(toks, heads)
    width, group = out_ref.shape
    lines = toks // 2
    line, side = lax.div(place.tok, 2), lax.rem(place.tok, 2)
    neighbour = (line * 2 + 1 - side, place.head)

    def line_at(k):
        return lax.rem(line + k + lines, lines)

    def peer(k):
        return (line_at(k) * 2 + side, place.head)

    keys = k_ref.shape[0]
    step_rows = math.gcd(keys, 512)
    steps = keys // step_rows

    def fetch(i):
        rows = pl.ds(pl.multiple_of(i * step_rows, step_rows), step_rows)
        return pltpu.make_async_copy(image_ref.at[rows], image.at[rows], image_sem.at[i])

    for i in range(steps):
        fetch(i).start()
    greet(place.head_peers() + [neighbour] + [peer(k) for k in range(1, lines)])
    gather = Gather(place, gather_refs)
    gather.start(layer_norm(tri_ref[...].astype(f32)).astype(bf16))
    vt_ref[:, head_size:, :] = jnp.ones((width // head_size, ONES, keys), bf16)

    def q_send(k):
        mine = queries.at[place.tok]
        return send(mine, mine, q_out.at[k], q_in.at[k], peer(-k) if k else neighbour)

    def q_arrival(k):
        slot = queries.at[line_at(k) * 2 + side]
        return send(slot, slot, q_out.at[k], q_in.at[k], peer(k))

    def project(i, carry):
        @pl.when(i == steps // 2)
        def _():
            gather.forward()

        @pl.when(i == steps * 3 // 4)
        def _():
            gather.finish()
            x = gather.rows[...].reshape(group, -1)
            product = jnp.transpose(dot(x, wq_ref[...]))
            queries[place.tok] = head_norm_rows(product, head_size, factor).astype(bf16)
            if lines > 1:
                q_send(1).start()

        rows = pl.ds(pl.multiple_of(i * step_rows, step_rows), step_rows)
        fetch(i).wait()
        x = image[rows, :]
        k = dot(x, wkv_ref[0])
        k_ref[rows, :] = (k * head_scale(k, head_size)).astype(bf16)
        v = jnp.transpose(dot(x, wkv_ref[1])).astype(bf16)
        vt_ref[:, :head_size, rows] = v.reshape(width // head_size, head_size, step_rows)
        return carry

    lax.fori_loop(0, steps, project, 0)
    for k in range(2, lines):
        q_send(k).start()
    q_send(0).start()

    def forward(k, slot):
        block = queries.at[slot]
        return send(block, block, f_out.at[k], f_in.at[k], neighbour)

    def pair_send(k, s):
        return send(tiles.at[s], pair_tiles.at[k], p_out.at[k], p_in.at[k], neighbour)

    def far_send(k):
        return send(joined.at[k], far_tiles.at[k], c_out.at[k], c_in.at[k], peer(k))

    def attend(s, carry):
        k = lax.div(s, 2) + 1
        last = k == lines
        first = lax.rem(s, 2) == 0
        mine = first != last
        slot = lax.rem(line + k, lines) * 2 + jnp.where(mine, side, 1 - side)

        @pl.when(jnp.logical_and(first, jnp.logical_not(last)))
        def _():
            block = queries.at[slot]
            send(block, block, q_out.at[k], q_in.at[k], neighbour).wait_recv()
            forward(k, slot).start()

        @pl.when(jnp.logical_and(jnp.logical_not(first), jnp.logical_not(last)))
        def _():
            forward(k, slot).wait_recv()

        @pl.when(jnp.logical_and(first, last))
        def _():
            block = queries.at[slot]
            send(block, block, q_out.at[0], q_in.at[0], neighbour).wait_recv()

        tiles[s] = attend_block(queries[slot], k_ref, vt_ref, head_size)

        @pl.when(jnp.logical_not(mine))
        def _():
            pair_send(k, s).start()

        @pl.when(jnp.logical_and(first, k > 1))
        def _():
            before = k - 1
            pair_send(before, s).wait_recv()
            joined[before] = pack(*join([tiles[2 * before - 2], pair_tiles[before]], width))
            far_send(before).start()

        return carry

    lax.fori_loop(0, 2 * lines, attend, 0)
    pair_send(lines, 0).wait_recv()
    for k in range(1, lines):
        far_send(k).wait_recv()
    mixed, totals = join(
        [tiles[2 * lines - 1], pair_tiles[lines]] + [far_tiles[k] for k in range(1, lines)], width
    )
    for h in range(width // head_size):
        rows = slice(h * head_size, (h + 1) * head_size)
        out_ref[rows, :] = (mixed[rows] / totals[h : h + 1]).astype(bf16)
    gather.drain()
    for k in range(lines):
        q_send(k).wait_send()
    for k in range(1, lines):
        forward(k, 0).wait_send()
        far_send(k).wait_send()
    for k in range(1, lines + 1):
        pair_send(k, 0).wait_send()


def cross(tri, image, wq, wkv, toks, heads, head_size, factor):
    rows, depth = tri.shape
    keys = image.shape[0]
    width = wq.shape[1]
    group = rows * heads
    lines = toks // 2
    tile = (width + 16, group)
    vmem = pl.BlockSpec(memory_space=pltpu.VMEM)
    dma = pltpu.SemaphoreType.DMA
    return pl.pallas_call(
        functools.partial(
            cross_kernel, toks=toks, heads=heads, head_size=head_size, factor=factor
        ),
        out_shape=jax.ShapeDtypeStruct((width, group), bf16),
        in_specs=[vmem, pl.BlockSpec(memory_space=pl.ANY), vmem, vmem],
        out_specs=vmem,
        scratch_shapes=[
            pltpu.VMEM((keys, depth), bf16),
            pltpu.VMEM((keys, width), bf16),
            pltpu.VMEM((width // head_size, head_size + ONES, keys), bf16),
            pltpu.VMEM((toks, width, group), bf16),
            pltpu.VMEM((2 * lines,) + tile, bf16),
            pltpu.VMEM((lines + 1,) + tile, bf16),
            pltpu.VMEM((lines,) + tile, bf16),
            pltpu.VMEM((lines,) + tile, bf16),
            dma((keys // math.gcd(keys, 512),)),
            dma((lines,)), dma((lines,)),
            dma((lines,)), dma((lines,)),
            dma((lines + 1,)), dma((lines + 1,)),
            dma((lines,)), dma((lines,)),
        ] + Gather.scratch(heads, rows, depth),
        compiler_params=pltpu.CompilerParams(
            vmem_limit_bytes=VMEM_LIMIT, collective_id=0, has_side_effects=True
        ),
        name="cross",
    )(tri, image, wq, wkv)


class Scatter:
    @staticmethod
    def scratch(heads, rows, depth):
        pairs = heads // 2
        dma = pltpu.SemaphoreType.DMA((pairs,))
        tiles = [pltpu.VMEM((pairs, rows, depth), bf16)] * 3
        return [pltpu.VMEM((pairs, 2, rows, depth), bf16)] + tiles + [dma] * 4

    def __init__(self, place, refs):
        self.place = place
        self.part, self.close, self.sums, self.distant = refs[:4]
        self.near_out, self.near_in, self.far_out, self.far_in = refs[4:]

    def near(self, k):
        p = self.place
        return send(
            self.part.at[k, 1 - p.core],
            self.close.at[k],
            self.near_out.at[k],
            self.near_in.at[k],
            p.partner(),
        )

    def far(self, k):
        return send(
            self.sums.at[k],
            self.distant.at[k],
            self.far_out.at[k],
            self.far_in.at[k],
            self.place.across(k),
        )

    def give(self, k, value):
        self.part[k] = value.reshape(self.part.shape[1:]).astype(bf16)
        self.near(k).start()

    def near_sum(self, k):
        self.near(k).wait_recv()
        return self.part[k, self.place.core].astype(f32) + self.close[k].astype(f32)

    def relay(self, k):
        self.sums[k] = self.near_sum(k).astype(bf16)
        self.far(k).start()

    def finish(self):
        total = self.near_sum(0)
        for k in range(1, self.place.pairs):
            self.far(k).wait_recv()
            total = total + self.distant[k].astype(f32)
        return total

    def drain(self):
        for k in range(self.place.pairs):
            self.near(k).wait_send()
        for k in range(1, self.place.pairs):
            self.far(k).wait_send()


def collect(place, scatter, mix, weight_ref):
    both = mix.shape[0] // place.pairs

    def partial(k):
        rows = pl.ds(pl.multiple_of(place.pair_at(k) * both, both), both)
        return dot(mix[rows, :], weight_ref[...])

    for k in range(1, place.pairs):
        scatter.give(k, partial(k))
    scatter.give(0, partial(0))
    for k in range(1, place.pairs):
        scatter.relay(k)
    return scatter.finish()


def self_kernel(
    tri_ref, mixed_ref, wout_ref, wqkv_ref, stream_ref, out_ref,
    mix, chunks, column, passed, k_ref, vt_ref, acc, results, landed,
    a_out, a_in, f_out, f_in, o_out, o_in, *refs,
    toks, heads, head_size, factor,
):
    place = Place(toks, heads)
    width, group = out_ref.shape
    count = width // head_size
    sharers = toks // count
    mine, part = lax.div(place.tok, sharers), lax.rem(place.tok, sharers)

    def owner(k):
        return lax.rem(mine + k + count, count)

    def owner_at(k):
        return (owner(k) * sharers + part, place.head)

    def sharer_at(m):
        return (mine * sharers + lax.rem(part + m, sharers), place.head)

    greet(
        place.head_peers()
        + [owner_at(k) for k in range(1, count)]
        + [sharer_at(m) for m in range(1, sharers)]
    )
    scatter = Scatter(place, refs[:8])
    gather = Gather(place, refs[8:])
    mix[...] = jnp.transpose(mixed_ref[...].astype(f32)).astype(bf16)
    vt_ref[head_size:, :] = jnp.ones((ONES, vt_ref.shape[1]), bf16)
    stream = tri_ref[...].astype(f32) + collect(place, scatter, mix, wout_ref)
    stream_ref[...] = stream
    gather.start(layer_norm(stream).astype(bf16))
    gather.forward()
    gather.finish()
    x = gather.rows[...].reshape(group, -1)
    for j in range(3):
        product = jnp.transpose(dot(x, wqkv_ref[j]))
        if j < 2:
            product = head_norm_rows(product, head_size, 1.0 if j else factor)
        chunks[:, j * head_size : (j + 1) * head_size, :] = product.reshape(
            count, head_size, group
        ).astype(bf16)

    def deal(k):
        return send(
            chunks.at[owner(k)], column.at[mine], a_out.at[k], a_in.at[k], owner_at(k)
        )

    def hand(k, m):
        source = column.at[owner(-k), pl.ds(head_size, 2 * head_size)]
        i = k * (sharers - 1) + m - 1
        return send(source, passed.at[k, m - 1], f_out.at[i], f_in.at[i], sharer_at(m))

    def fill(n, chunk):
        rows = slice(n * group, (n + 1) * group)
        k_ref[rows, :] = jnp.transpose(chunk[:head_size].astype(f32)).astype(bf16)
        vt_ref[:head_size, rows] = chunk[head_size:]

    for k in range(1, count):
        deal(k).start()
    column[mine] = chunks[mine]
    for k in range(count):
        if k:
            deal(k).wait_recv()
        for m in range(1, sharers):
            hand(k, m).start()
        fill(k, column[owner(-k), head_size:])

    def give_back(j):
        return send(results.at[j], landed.at[mine], o_out.at[j], o_in.at[j], owner_at(j + 1))

    span = count * group
    for m in range(sharers):
        if m:
            for k in range(count):
                hand(k, m).wait_recv()
                fill(m * count + k, passed[k, m - 1])
        keys = slice(m * span, (m + 1) * span)
        for j in range(count):
            scores = dot(k_ref[keys, :], column[owner(j + 1), :head_size])
            total = dot(vt_ref[:, keys], jnp.exp2(scores).astype(bf16))
            if m:
                total = acc[j] + total
            if m < sharers - 1:
                acc[j] = total
                continue
            result = (total[:head_size] / total[head_size : head_size + 1]).astype(bf16)
            if j == count - 1:
                landed[mine] = result
            else:
                results[j] = result
                give_back(j).start()
    for j in range(count - 1):
        give_back(j).wait_recv()
    out_ref[...] = landed[...].reshape(width, group)
    scatter.drain()
    gather.drain()
    for k in range(1, count):
        deal(k).wait_send()
    for k in range(count):
        for m in range(1, sharers):
            hand(k, m).wait_send()
    for j in range(count - 1):
        give_back(j).wait_send()


def self_stage(tri, mixed, wout, wqkv, toks, heads, head_size, factor):
    rows, depth = tri.shape
    width, group = mixed.shape
    count = width // head_size
    sharers = toks // count
    vmem = pl.BlockSpec(memory_space=pltpu.VMEM)
    dma = pltpu.SemaphoreType.DMA
    passes = max(1, count * (sharers - 1))
    return pl.pallas_call(
        functools.partial(
            self_kernel, toks=toks, heads=heads, head_size=head_size, factor=factor
        ),
        out_shape=[
            jax.ShapeDtypeStruct((rows, depth), f32),
            jax.ShapeDtypeStruct((width, group), bf16),
        ],
        in_specs=[vmem] * 4,
        out_specs=[vmem] * 2,
        scratch_shapes=[
            pltpu.VMEM((group, width), bf16),
            pltpu.VMEM((count, 3 * head_size, group), bf16),
            pltpu.VMEM((count, 3 * head_size, group), bf16),
            pltpu.VMEM((count, max(1, sharers - 1), 2 * head_size, group), bf16),
            pltpu.VMEM((toks * group, head_size), bf16),
            pltpu.VMEM((head_size + ONES, toks * group), bf16),
            pltpu.VMEM((count, head_size + ONES, group), f32),
            pltpu.VMEM((count, head_size, group), bf16),
            pltpu.VMEM((count, head_size, group), bf16),
            dma((count,)), dma((count,)),
            dma((passes,)), dma((passes,)),
            dma((count,)), dma((count,)),
        ] + Scatter.scratch(heads, rows, depth) + Gather.scratch(heads, rows, depth),
        compiler_params=pltpu.CompilerParams(
            vmem_limit_bytes=VMEM_LIMIT, collective_id=1, has_side_effects=True
        ),
        name="self_stage",
    )(tri, mixed, wout, wqkv)


def mlp_kernel(
    stream_ref, mixed_ref, wout_ref, win_ref, wdown_ref, out_ref, mix, *refs, toks, heads
):
    place = Place(toks, heads)
    greet(place.head_peers())
    scatter = Scatter(place, refs[:8])
    second = Scatter(place, refs[8:16])
    gather = Gather(place, refs[16:])
    mix[...] = jnp.transpose(mixed_ref[...].astype(f32)).astype(bf16)
    stream = stream_ref[...] + collect(place, scatter, mix, wout_ref)
    gather.start(layer_norm(stream).astype(bf16))

    def mlp(k):
        x = gather.rows[pl.ds(place.pair_at(k) * 2, 2)].reshape(-1, stream.shape[1])
        hidden = jax.nn.gelu(dot(x, win_ref[...]), approximate=True).astype(bf16)
        second.give(k, dot(hidden, wdown_ref[...]))

    gather.near_arrival(0).wait_recv()
    mlp(0)
    gather.forward()
    for k in range(1, place.pairs):
        gather.near_arrival(k).wait_recv()
    for k in range(1, place.pairs):
        mlp(k)
    for k in range(1, place.pairs):
        second.relay(k)
    out_ref[...] = (stream + second.finish()).astype(bf16)
    scatter.drain()
    second.drain()
    gather.drain()


def mlp_stage(stream, mixed, wout, win, wdown, toks, heads):
    rows, depth = stream.shape
    width, group = mixed.shape
    vmem = pl.BlockSpec(memory_space=pltpu.VMEM)
    return pl.pallas_call(
        functools.partial(mlp_kernel, toks=toks, heads=heads),
        out_shape=jax.ShapeDtypeStruct((rows, depth), bf16),
        in_specs=[vmem] * 5,
        out_specs=vmem,
        scratch_shapes=[pltpu.VMEM((group, width), bf16)]
        + Scatter.scratch(heads, rows, depth) * 2
        + Gather.scratch(heads, rows, depth),
        compiler_params=pltpu.CompilerParams(
            vmem_limit_bytes=VMEM_LIMIT, collective_id=2, has_side_effects=True
        ),
        name="mlp_stage",
    )(stream, mixed, wout, win, wdown)


def per_device(
    tri_tokens, image_tokens, cross_q, cross_kv, cross_out, self_qkv, self_out, mlp_in, mlp_out,
    *, tok, head
):
    head_size = tri_tokens.shape[1] // HEADS
    factor = score_gain / math.sqrt(head_size) * math.log2(math.e)
    mixed = cross(tri_tokens, image_tokens, cross_q, cross_kv, tok, head, head_size, factor)
    stream, mixed = self_stage(
        tri_tokens, mixed, cross_out, self_qkv, tok, head, head_size, factor
    )
    return mlp_stage(stream, mixed, self_out, mlp_in, mlp_out, tok, head)


def solution(mesh):
    return jax.shard_map(
        functools.partial(per_device, tok=mesh.shape["tok"], head=mesh.shape["head"]),
        mesh=mesh,
        in_specs=(
            P(("tok", "head"), None),
            P("tok", None),
            P(None, "head"),
            P(None, None, "head"),
            P("head", None),
            P(None, None, "head"),
            P("head", None),
            P(None, "head"),
            P("head", None),
        ),
        out_specs=P(("tok", "head"), None),
        check_vma=False,
    )
```

```python
import functools
import math

import jax
import jax.numpy as jnp
from jax import lax
from jax.experimental import pallas as pl
from jax.experimental.pallas import tpu as pltpu
from jax.sharding import PartitionSpec as P

HEADS = 16
score_gain = 2.5
VMEM_LIMIT = 60 << 20
MESH = pl.DeviceIdType.MESH
ONES = 16
FORWARD_AT = 2
QUERY_AT = 3
bf16 = jnp.bfloat16
f32 = jnp.float32


def layer_norm(values):
    centered = values - jnp.mean(values, axis=-1, keepdims=True)
    return centered * lax.rsqrt(jnp.mean(centered * centered, axis=-1, keepdims=True) + 1e-05)


def dot(a, b):
    return jnp.dot(a, b, preferred_element_type=f32)


def head_scale(product, head_size):
    width = product.shape[1]
    rows = lax.broadcasted_iota(jnp.int32, (width, width), 0) // head_size
    cols = lax.broadcasted_iota(jnp.int32, (width, width), 1) // head_size
    same = (rows == cols).astype(f32).astype(bf16)
    squares = product * product
    high = squares.astype(bf16)
    low = (squares - high.astype(f32)).astype(bf16)
    total = dot(high, same) + dot(low, same)
    return lax.rsqrt(total * (1.0 / head_size) + 1e-06)


def head_norm_rows(product, head_size, factor):
    width, count = product.shape
    shaped = product.reshape(width // head_size, head_size, count)
    mean = jnp.sum(shaped * shaped, axis=1, keepdims=True) * (1.0 / head_size)
    return (shaped * (lax.rsqrt(mean + 1e-06) * factor)).reshape(width, count)


def send(source, target, send_sem, recv_sem, device):
    copy = pltpu.make_async_remote_copy(
        src_ref=source,
        dst_ref=target,
        send_sem=send_sem,
        recv_sem=recv_sem,
        device_id=device,
        device_id_type=MESH,
    )
    return copy


def greet(devices):
    barrier = pltpu.get_barrier_semaphore()
    for device in devices:
        pl.semaphore_signal(barrier, inc=1, device_id=device, device_id_type=MESH)
    pl.semaphore_wait(barrier, len(devices))


class Place:
    def __init__(self, toks, heads):
        self.toks, self.heads = toks, heads
        self.tok, self.head = lax.axis_index("tok"), lax.axis_index("head")
        self.pairs = heads // 2
        self.pair, self.core = lax.div(self.head, 2), lax.rem(self.head, 2)

    def partner(self):
        return (self.tok, self.pair * 2 + 1 - self.core)

    def pair_at(self, k):
        return lax.rem(self.pair + k + self.pairs, self.pairs)

    def across(self, k):
        return (self.tok, self.pair_at(k) * 2 + self.core)

    def head_peers(self):
        return [self.partner()] + [self.across(k) for k in range(1, self.pairs)]


class Gather:
    @staticmethod
    def scratch(heads, rows, depth):
        dma = pltpu.SemaphoreType.DMA((heads // 2,))
        return [pltpu.VMEM((heads, rows, depth), bf16), dma, dma, dma, dma]

    def __init__(self, place, refs):
        self.place = place
        self.rows, self.pair_out, self.pair_in, self.far_out, self.far_in = refs

    def far(self, k):
        p = self.place
        mine = self.rows.at[p.head]
        return send(mine, mine, self.far_out.at[k], self.far_in.at[k], p.across(k))

    def far_arrival(self, k):
        p = self.place
        slot = self.rows.at[p.pair_at(-k) * 2 + p.core]
        return send(slot, slot, self.far_out.at[k], self.far_in.at[k], p.across(-k))

    def near(self, k):
        p = self.place
        slot = self.rows.at[p.pair_at(-k) * 2 + p.core]
        return send(slot, slot, self.pair_out.at[k], self.pair_in.at[k], p.partner())

    def near_arrival(self, k):
        p = self.place
        slot = self.rows.at[p.pair_at(-k) * 2 + 1 - p.core]
        return send(slot, slot, self.pair_out.at[k], self.pair_in.at[k], p.partner())

    def start(self, value):
        self.rows[self.place.head] = value
        for k in range(1, self.place.pairs):
            self.far(k).start()
        self.near(0).start()

    def forward(self):
        for k in range(1, self.place.pairs):
            self.far_arrival(k).wait_recv()
            self.near(k).start()

    def finish(self):
        for k in range(self.place.pairs):
            self.near_arrival(k).wait_recv()

    def drain(self):
        for k in range(1, self.place.pairs):
            self.far(k).wait_send()
        for k in range(self.place.pairs):
            self.near(k).wait_send()


def join(tiles, width):
    total = functools.reduce(lambda a, b: a + b, [t.astype(f32) for t in tiles])
    return total[:width], total[width : width + 8] + total[width + 8 : width + 16]


def pack(mixed, totals):
    high = totals.astype(bf16).astype(f32)
    return jnp.concatenate([mixed, high, totals - high], axis=0).astype(bf16)


def attend_block(queries, k_ref, vt_ref, head_size):
    width, count = queries.shape
    lanes = min(128, width)
    keys = k_ref.shape[0]
    block = math.gcd(keys, 2048)
    row = lax.broadcasted_iota(jnp.int32, (lanes, count), 0) // head_size
    place = lax.broadcasted_iota(jnp.int32, (ONES, count), 0) % 8
    mixed, totals = [], jnp.zeros((ONES, count), f32)
    for h in range(width // head_size):
        first = h * head_size // lanes * lanes
        picked = queries[first : first + lanes]
        if lanes > head_size:
            picked = jnp.where(row == h % (lanes // head_size), picked, jnp.zeros_like(picked))
        acc = jnp.zeros((head_size + ONES, count), f32)
        for i in range(keys // block):
            rows = slice(i * block, (i + 1) * block)
            scores = dot(k_ref[rows, first : first + lanes], picked)
            acc = acc + dot(vt_ref[h, :, rows], jnp.exp2(scores).astype(bf16))
        mixed.append(acc[:head_size])
        totals = jnp.where(place == h, acc[head_size:], totals)
    return pack(jnp.concatenate(mixed, axis=0), totals[:8])


class Share:
    @staticmethod
    def scratch(count, heads):
        dma = pltpu.SemaphoreType.DMA((count * (heads // 2),))
        return [dma, dma, dma, dma, pltpu.SemaphoreType.DMA((count,))]

    def __init__(self, place, own, full, sems):
        self.place, self.own, self.full = place, own, full
        self.far_out, self.far_in, self.near_out, self.near_in, self.local_sem = sems

    def far(self, i, k):
        p = self.place
        n = i * p.pairs + k
        return send(
            self.own[i], self.full[i](p.head), self.far_out.at[n], self.far_in.at[n], p.across(k)
        )

    def near(self, i, k):
        p = self.place
        n = i * p.pairs + k
        slot = self.full[i](p.pair_at(-k) * 2 + p.core)
        source = slot if k else self.own[i]
        return send(source, slot, self.near_out.at[n], self.near_in.at[n], p.partner())

    def local(self, i):
        return pltpu.make_async_copy(
            self.own[i], self.full[i](self.place.head), self.local_sem.at[i]
        )

    def start(self, i):
        for k in range(1, self.place.pairs):
            self.far(i, k).start()
        self.near(i, 0).start()
        self.local(i).start()

    def forward(self, i):
        for k in range(1, self.place.pairs):
            self.far(i, k).wait_recv()
            self.near(i, k).start()

    def finish(self, i):
        self.local(i).wait()
        for k in range(self.place.pairs):
            self.near(i, k).wait()
        for k in range(1, self.place.pairs):
            self.far(i, k).wait_send()


def pick(step, values):
    chosen = jnp.int32(values[0])
    for i, value in enumerate(values):
        chosen = jnp.where(step == i, jnp.int32(value), chosen)
    return chosen


def block_order(lines):
    order = sorted(range(1, lines), key=lambda k: (-min(k, lines - k), k))
    turns = [(False, lines)]
    for k in order[:-1]:
        turns += [(True, k), (False, k)]
    for k in order[-1:]:
        turns += [(False, k), (True, k)]
    turns.append((True, lines))
    take, combine = {}, {}
    for j, k in enumerate(order):
        if j == 0:
            take.setdefault(0, []).append(k)
        elif j == len(order) - 1:
            take.setdefault(turns.index((False, order[j - 1])), []).append(k)
        else:
            take.setdefault(turns.index((True, k)), []).append(k)
        after = turns.index((True, k)) if j == len(order) - 1 else turns.index((False, k)) + 1
        combine.setdefault(after, []).append(k)
    return order, turns, take, combine


def cross_kernel(
    tri_ref, image_ref, wq_ref, wkv_ref, *rest,
    toks, heads, head_size, factor, shared,
):
    own_refs, out_ref, full_refs = rest[:shared], rest[shared], rest[shared + 1 : 2 * shared + 1]
    cross_body(
        tri_ref, image_ref, wq_ref, wkv_ref, own_refs, out_ref, full_refs,
        *rest[2 * shared + 1 :], toks=toks, heads=heads, head_size=head_size, factor=factor,
    )


def cross_body(
    tri_ref, image_ref, wq_ref, wkv_ref, own_refs, out_ref, full_refs,
    image, k_ref, vt_ref, queries, tiles, pair_tiles, joined, far_tiles,
    image_sem, q_out, q_in, f_out, f_in, p_out, p_in, c_out, c_in, *refs,
    toks, heads, head_size, factor,
):
    place = Place(toks, heads)
    _, width, rows_each = out_ref.shape
    group = rows_each * heads
    lines = toks // 2
    order, turns, take, combine = block_order(lines)
    line, side = lax.div(place.tok, 2), lax.rem(place.tok, 2)
    neighbour = (line * 2 + 1 - side, place.head)

    def line_at(k):
        return lax.rem(line + k + lines, lines)

    def peer(k):
        return (line_at(k) * 2 + side, place.head)

    keys = k_ref.shape[0]
    step_rows = math.gcd(keys, 512)
    steps = keys // step_rows

    def fetch(i):
        rows = pl.ds(pl.multiple_of(i * step_rows, step_rows), step_rows)
        return pltpu.make_async_copy(image_ref.at[rows], image.at[rows], image_sem.at[i])

    for i in range(steps):
        fetch(i).start()
    greet(place.head_peers() + [neighbour] + [peer(k) for k in range(1, lines)])
    gather = Gather(place, refs[:5])
    own, full = [], []
    for mine, whole in zip(own_refs, full_refs):
        for j in range(mine.shape[0]):
            own.append(mine.at[j])
            full.append(functools.partial(lambda slot, whole, j: whole.at[slot, j], whole=whole, j=j))
    share = Share(place, own, full, refs[5:]) if own else None
    gather.start(layer_norm(tri_ref[...].astype(f32)).astype(bf16))
    vt_ref[:, head_size:, :] = jnp.ones((width // head_size, ONES, keys), bf16)

    def q_send(k):
        mine = queries.at[place.tok]
        return send(mine, mine, q_out.at[k], q_in.at[k], peer(-k) if k else neighbour)

    def q_arrival(k):
        slot = queries.at[line_at(k) * 2 + side]
        return send(slot, slot, q_out.at[k], q_in.at[k], peer(k))

    def project(i, carry):
        @pl.when(i == FORWARD_AT * steps // 8)
        def _():
            gather.forward()

        @pl.when(i == QUERY_AT * steps // 8)
        def _():
            gather.finish()
            x = gather.rows[...].reshape(group, -1)
            product = jnp.transpose(dot(x, wq_ref[...]))
            queries[place.tok] = head_norm_rows(product, head_size, factor).astype(bf16)
            q_send(0).start()
            for k in order:
                q_send(k).start()
            for n in range(min(2, len(own))):
                share.start(n)

        rows = pl.ds(pl.multiple_of(i * step_rows, step_rows), step_rows)
        fetch(i).wait()
        x = image[rows, :]
        k = dot(x, wkv_ref[0])
        k_ref[rows, :] = (k * head_scale(k, head_size)).astype(bf16)
        v = jnp.transpose(dot(x, wkv_ref[1])).astype(bf16)
        vt_ref[:, :head_size, rows] = v.reshape(width // head_size, head_size, step_rows)
        return carry

    lax.fori_loop(0, steps, project, 0)
    def forward(k, slot):
        block = queries.at[slot]
        return send(block, block, f_out.at[k], f_in.at[k], neighbour)

    def pair_send(k, s):
        return send(tiles.at[s], pair_tiles.at[k], p_out.at[k], p_in.at[k], neighbour)

    def far_send(k):
        return send(joined.at[k], far_tiles.at[k], c_out.at[k], c_in.at[k], peer(k))

    def turn_of(n):
        return min(len(turns) - 2, max(0, n - 3))

    def arrive(k):
        slot = lax.rem(line + k, lines) * 2 + side
        block = queries.at[slot]
        send(block, block, q_out.at[k], q_in.at[k], neighbour).wait_recv()
        forward(k, slot).start()

    def before(i):
        mine, k = turns[i]
        if not mine and k == lines:
            block = queries.at[line * 2 + 1 - side]
            send(block, block, q_out.at[0], q_in.at[0], neighbour).wait_recv()
        for taken in take.get(i, []):
            arrive(taken)
        if not mine and k < lines:
            forward(k, lax.rem(line + k, lines) * 2 + 1 - side).wait_recv()
        if own:
            for n in range(2, len(own)):
                if i == turn_of(n):
                    share.start(n)

    def after(i):
        mine, k = turns[i]
        if not mine:
            pair_send(k, i).start()
        for done in combine.get(i, []):
            pair_send(done, i).wait_recv()
            joined[done] = pack(
                *join([tiles[turns.index((True, done))], pair_tiles[done]], width)
            )
            far_send(done).start()
        if own:
            for n in range(len(own)):
                if i == min(len(turns) - 1, turn_of(n) + 1):
                    share.forward(n)

    def attend(s, carry):
        for i in range(len(turns)):
            pl.when(s == i)(functools.partial(before, i))
        k = pick(s, [k for _, k in turns])
        mine = pick(s, [int(m) for m, _ in turns])
        slot = lax.rem(line + k, lines) * 2 + mine * side + (1 - mine) * (1 - side)
        tiles[s] = attend_block(queries[slot], k_ref, vt_ref, head_size)
        for i in range(len(turns)):
            pl.when(s == i)(functools.partial(after, i))
        return carry

    lax.fori_loop(0, len(turns), attend, 0)
    pair_send(lines, 0).wait_recv()
    for k in range(1, lines):
        far_send(k).wait_recv()
    mixed, totals = join(
        [tiles[2 * lines - 1], pair_tiles[lines]] + [far_tiles[k] for k in range(1, lines)], width
    )
    for h in range(width // head_size):
        rows = slice(h * head_size, (h + 1) * head_size)
        mix = (mixed[rows] / totals[h : h + 1]).astype(bf16)
        for n in range(heads):
            out_ref[n, rows, :] = mix[:, n * rows_each : (n + 1) * rows_each]
    gather.drain()
    for k in range(lines):
        q_send(k).wait_send()
    for k in range(1, lines):
        forward(k, 0).wait_send()
        far_send(k).wait_send()
    for k in range(1, lines + 1):
        pair_send(k, 0).wait_send()
    for n in range(len(own)):
        share.finish(n)


def cross(tri, image, wq, wkv, weights, toks, heads, head_size, factor):
    rows, depth = tri.shape
    keys = image.shape[0]
    width = wq.shape[1]
    group = rows * heads
    lines = toks // 2
    tile = (width + 16, group)
    vmem = pl.BlockSpec(memory_space=pltpu.VMEM)
    anywhere = pl.BlockSpec(memory_space=pl.ANY)
    pieces = sum(w.shape[0] for w in weights)
    dma = pltpu.SemaphoreType.DMA
    return pl.pallas_call(
        functools.partial(
            cross_kernel, toks=toks, heads=heads, head_size=head_size, factor=factor,
            shared=len(weights),
        ),
        out_shape=[jax.ShapeDtypeStruct((heads, width, rows), bf16)]
        + [jax.ShapeDtypeStruct((heads,) + w.shape, bf16) for w in weights],
        in_specs=[vmem, anywhere, vmem, vmem] + [anywhere] * len(weights),
        out_specs=[vmem] + [anywhere] * len(weights),
        scratch_shapes=[
            pltpu.VMEM((keys, depth), bf16),
            pltpu.VMEM((keys, width), bf16),
            pltpu.VMEM((width // head_size, head_size + ONES, keys), bf16),
            pltpu.VMEM((toks, width, group), bf16),
            pltpu.VMEM((2 * lines,) + tile, bf16),
            pltpu.VMEM((lines + 1,) + tile, bf16),
            pltpu.VMEM((lines,) + tile, bf16),
            pltpu.VMEM((lines,) + tile, bf16),
            dma((keys // math.gcd(keys, 512),)),
            dma((lines,)), dma((lines,)),
            dma((lines,)), dma((lines,)),
            dma((lines + 1,)), dma((lines + 1,)),
            dma((lines,)), dma((lines,)),
        ]
        + Gather.scratch(heads, rows, depth)
        + (Share.scratch(pieces, heads) if weights else []),
        compiler_params=pltpu.CompilerParams(
            vmem_limit_bytes=VMEM_LIMIT, collective_id=0, has_side_effects=True
        ),
        name="cross",
    )(tri, image, wq, wkv, *weights)


class Scatter:
    @staticmethod
    def scratch(heads, rows, depth):
        pairs = heads // 2
        dma = pltpu.SemaphoreType.DMA((pairs,))
        tiles = [pltpu.VMEM((pairs, rows, depth), bf16)] * 3
        return [pltpu.VMEM((pairs, 2, rows, depth), bf16)] + tiles + [dma] * 4

    def __init__(self, place, refs):
        self.place = place
        self.part, self.close, self.sums, self.distant = refs[:4]
        self.near_out, self.near_in, self.far_out, self.far_in = refs[4:]

    def near(self, k):
        p = self.place
        return send(
            self.part.at[k, 1 - p.core],
            self.close.at[k],
            self.near_out.at[k],
            self.near_in.at[k],
            p.partner(),
        )

    def far(self, k):
        return send(
            self.sums.at[k],
            self.distant.at[k],
            self.far_out.at[k],
            self.far_in.at[k],
            self.place.across(k),
        )

    def give(self, k, value):
        self.part[k] = value.reshape(self.part.shape[1:]).astype(bf16)
        self.near(k).start()

    def near_sum(self, k):
        self.near(k).wait_recv()
        return self.part[k, self.place.core].astype(f32) + self.close[k].astype(f32)

    def relay(self, k):
        self.sums[k] = self.near_sum(k).astype(bf16)
        self.far(k).start()

    def finish(self):
        total = self.near_sum(0)
        for k in range(1, self.place.pairs):
            self.far(k).wait_recv()
            total = total + self.distant[k].astype(f32)
        return total

    def drain(self):
        for k in range(self.place.pairs):
            self.near(k).wait_send()
        for k in range(1, self.place.pairs):
            self.far(k).wait_send()


def collect(place, scatter, mix, weight_ref):
    both = mix.shape[0] // place.pairs

    def partial(k):
        rows = pl.ds(pl.multiple_of(place.pair_at(k) * both, both), both)
        return dot(mix[rows, :], weight_ref[...])

    for k in range(1, place.pairs):
        scatter.give(k, partial(k))
    scatter.give(0, partial(0))
    for k in range(1, place.pairs):
        scatter.relay(k)
    return scatter.finish()


def self_kernel(
    tri_ref, mixed_ref, wout_ref, wqkv_ref, stream_ref, out_ref,
    mix, chunks, column, passed, k_ref, vt_ref, acc, results, landed,
    a_out, a_in, f_out, f_in, o_out, o_in, *refs,
    toks, heads, head_size, factor,
):
    place = Place(toks, heads)
    width, group = out_ref.shape
    count = width // head_size
    sharers = toks // count
    mine, part = lax.div(place.tok, sharers), lax.rem(place.tok, sharers)

    def owner(k):
        return lax.rem(mine + k + count, count)

    def owner_at(k):
        return (owner(k) * sharers + part, place.head)

    def sharer_at(m):
        return (mine * sharers + lax.rem(part + m, sharers), place.head)

    greet(
        place.head_peers()
        + [owner_at(k) for k in range(1, count)]
        + [sharer_at(m) for m in range(1, sharers)]
    )
    scatter = Scatter(place, refs[:8])
    gather = Gather(place, refs[8:])
    mix[...] = jnp.transpose(mixed_ref[...].astype(f32)).astype(bf16)
    vt_ref[head_size:, :] = jnp.ones((ONES, vt_ref.shape[1]), bf16)
    stream = tri_ref[...].astype(f32) + collect(place, scatter, mix, wout_ref)
    stream_ref[...] = stream
    gather.start(layer_norm(stream).astype(bf16))
    gather.forward()
    gather.finish()
    x = gather.rows[...].reshape(group, -1)
    for j in range(3):
        product = jnp.transpose(dot(x, wqkv_ref[j]))
        if j < 2:
            product = head_norm_rows(product, head_size, 1.0 if j else factor)
        chunks[:, j * head_size : (j + 1) * head_size, :] = product.reshape(
            count, head_size, group
        ).astype(bf16)

    def deal(k):
        return send(
            chunks.at[owner(k)], column.at[mine], a_out.at[k], a_in.at[k], owner_at(k)
        )

    def hand(k, m):
        source = column.at[owner(-k), pl.ds(head_size, 2 * head_size)]
        i = k * (sharers - 1) + m - 1
        return send(source, passed.at[k, m - 1], f_out.at[i], f_in.at[i], sharer_at(m))

    def fill(n, chunk):
        rows = slice(n * group, (n + 1) * group)
        k_ref[rows, :] = jnp.transpose(chunk[:head_size].astype(f32)).astype(bf16)
        vt_ref[:head_size, rows] = chunk[head_size:]

    for k in range(1, count):
        deal(k).start()
    column[mine] = chunks[mine]
    for k in range(count):
        if k:
            deal(k).wait_recv()
        for m in range(1, sharers):
            hand(k, m).start()
        fill(k, column[owner(-k), head_size:])

    def give_back(j):
        return send(results.at[j], landed.at[mine], o_out.at[j], o_in.at[j], owner_at(j + 1))

    span = count * group
    for m in range(sharers):
        if m:
            for k in range(count):
                hand(k, m).wait_recv()
                fill(m * count + k, passed[k, m - 1])
        keys = slice(m * span, (m + 1) * span)
        for j in range(count):
            scores = dot(k_ref[keys, :], column[owner(j + 1), :head_size])
            total = dot(vt_ref[:, keys], jnp.exp2(scores).astype(bf16))
            if m:
                total = acc[j] + total
            if m < sharers - 1:
                acc[j] = total
                continue
            result = (total[:head_size] / total[head_size : head_size + 1]).astype(bf16)
            if j == count - 1:
                landed[mine] = result
            else:
                results[j] = result
                give_back(j).start()
    for j in range(count - 1):
        give_back(j).wait_recv()
    out_ref[...] = landed[...].reshape(width, group)
    scatter.drain()
    gather.drain()
    for k in range(1, count):
        deal(k).wait_send()
    for k in range(count):
        for m in range(1, sharers):
            hand(k, m).wait_send()
    for j in range(count - 1):
        give_back(j).wait_send()


def self_stage(tri, mixed, wout, wqkv, toks, heads, head_size, factor):
    rows, depth = tri.shape
    width, group = mixed.shape
    count = width // head_size
    sharers = toks // count
    vmem = pl.BlockSpec(memory_space=pltpu.VMEM)
    dma = pltpu.SemaphoreType.DMA
    passes = max(1, count * (sharers - 1))
    return pl.pallas_call(
        functools.partial(
            self_kernel, toks=toks, heads=heads, head_size=head_size, factor=factor
        ),
        out_shape=[
            jax.ShapeDtypeStruct((rows, depth), f32),
            jax.ShapeDtypeStruct((width, group), bf16),
        ],
        in_specs=[vmem] * 4,
        out_specs=[vmem] * 2,
        scratch_shapes=[
            pltpu.VMEM((group, width), bf16),
            pltpu.VMEM((count, 3 * head_size, group), bf16),
            pltpu.VMEM((count, 3 * head_size, group), bf16),
            pltpu.VMEM((count, max(1, sharers - 1), 2 * head_size, group), bf16),
            pltpu.VMEM((toks * group, head_size), bf16),
            pltpu.VMEM((head_size + ONES, toks * group), bf16),
            pltpu.VMEM((count, head_size + ONES, group), f32),
            pltpu.VMEM((count, head_size, group), bf16),
            pltpu.VMEM((count, head_size, group), bf16),
            dma((count,)), dma((count,)),
            dma((passes,)), dma((passes,)),
            dma((count,)), dma((count,)),
        ] + Scatter.scratch(heads, rows, depth) + Gather.scratch(heads, rows, depth),
        compiler_params=pltpu.CompilerParams(
            vmem_limit_bytes=VMEM_LIMIT, collective_id=1, has_side_effects=True
        ),
        name="self_stage",
    )(tri, mixed, wout, wqkv)


def mlp_kernel(
    stream_ref, mixed_ref, wout_ref, win_ref, wdown_ref, out_ref, mix, *refs, toks, heads
):
    place = Place(toks, heads)
    greet(place.head_peers())
    scatter = Scatter(place, refs[:8])
    second = Scatter(place, refs[8:16])
    gather = Gather(place, refs[16:])
    mix[...] = jnp.transpose(mixed_ref[...].astype(f32)).astype(bf16)
    stream = stream_ref[...] + collect(place, scatter, mix, wout_ref)
    gather.start(layer_norm(stream).astype(bf16))

    def mlp(k):
        x = gather.rows[pl.ds(place.pair_at(k) * 2, 2)].reshape(-1, stream.shape[1])
        hidden = jax.nn.gelu(dot(x, win_ref[...]), approximate=True).astype(bf16)
        second.give(k, dot(hidden, wdown_ref[...]))

    gather.near_arrival(0).wait_recv()
    mlp(0)
    gather.forward()
    for k in range(1, place.pairs):
        gather.near_arrival(k).wait_recv()
    for k in range(1, place.pairs):
        mlp(k)
    for k in range(1, place.pairs):
        second.relay(k)
    out_ref[...] = (stream + second.finish()).astype(bf16)
    scatter.drain()
    second.drain()
    gather.drain()


def mlp_stage(stream, mixed, wout, win, wdown, toks, heads):
    rows, depth = stream.shape
    width, group = mixed.shape
    vmem = pl.BlockSpec(memory_space=pltpu.VMEM)
    return pl.pallas_call(
        functools.partial(mlp_kernel, toks=toks, heads=heads),
        out_shape=jax.ShapeDtypeStruct((rows, depth), bf16),
        in_specs=[vmem] * 5,
        out_specs=vmem,
        scratch_shapes=[pltpu.VMEM((group, width), bf16)]
        + Scatter.scratch(heads, rows, depth) * 2
        + Gather.scratch(heads, rows, depth),
        compiler_params=pltpu.CompilerParams(
            vmem_limit_bytes=VMEM_LIMIT, collective_id=2, has_side_effects=True
        ),
        name="mlp_stage",
    )(stream, mixed, wout, win, wdown)


def late_kernel(
    tri_ref, mixed_ref, cross_out_ref, qkv_ref, self_out_ref, win_ref, wdown_ref, out_ref,
    cross_out, qkv, self_out, win, down, mixes, chunks, column, passed, k_ref, vt_ref, acc,
    results, landed, load_sem, m_out, m_in, a_out, a_in, f_out, f_in, r_out, r_in, *refs,
    toks, heads, head_size, factor,
):
    place = Place(toks, heads)
    rows, depth = tri_ref.shape
    width = mixed_ref.shape[1]
    count = width // head_size
    sharers = toks // count
    sources = count * heads
    mine, part = lax.div(place.tok, sharers), lax.rem(place.tok, sharers)
    every = [(a, h) for h in range(heads) for a in range(count)]

    def owner(a):
        return lax.rem(mine + a + count, count)

    def column_at(h):
        return lax.rem(place.head + h + heads, heads)

    def device_at(a, h):
        return (owner(a) * sharers + part, column_at(h))

    def sharer_at(m):
        return (mine * sharers + lax.rem(part + m, sharers), place.head)

    def load(i):
        source, target = [
            (cross_out_ref, cross_out), (qkv_ref, qkv), (self_out_ref, self_out),
            (win_ref, win), (wdown_ref, down),
        ][i]
        return pltpu.make_async_copy(source, target, load_sem.at[i])

    for i in range(5):
        load(i).start()
    greet(
        [device_at(a, h) for a, h in every if (a, h) != (0, 0)]
        + [sharer_at(m) for m in range(1, sharers)]
    )
    scatter = Scatter(place, refs[:8])
    gather = Gather(place, refs[8:])

    def swap(h):
        return send(
            mixed_ref.at[column_at(h)], mixes.at[place.head], m_out.at[h], m_in.at[h],
            device_at(0, h),
        )

    for h in range(1, heads):
        swap(h).start()
    mixes[place.head] = mixed_ref[place.head]
    vt_ref[head_size:, :] = jnp.ones((ONES, vt_ref.shape[1]), bf16)
    load(0).wait()
    for h in range(1, heads):
        swap(h).wait_recv()

    def turned(ref):
        return jnp.transpose(ref[...].reshape(-1, rows).astype(f32)).astype(bf16)

    stream = tri_ref[...].astype(f32) + dot(turned(mixes), cross_out[...].reshape(-1, depth))
    x = layer_norm(stream).astype(bf16)
    load(1).wait()

    def deal(a, h):
        i = a * heads + h
        return send(
            chunks.at[column_at(h), owner(a)],
            column.at[mine * heads + place.head],
            a_out.at[i], a_in.at[i], device_at(a, h),
        )

    def project(h):
        n = column_at(h)
        for j in range(3):
            product = jnp.transpose(dot(x, qkv[n, j]))
            if j < 2:
                product = head_norm_rows(product, head_size, 1.0 if j else factor)
            chunks[n, :, j * head_size : (j + 1) * head_size, :] = product.reshape(
                count, head_size, rows
            ).astype(bf16)

    for h in range(heads):
        project(h)
        for a in sorted(range(count), key=lambda a: -min(a, count - a)):
            if (a, h) != (0, 0):
                deal(a, h).start()
    column[mine * heads + place.head] = chunks[place.head, mine]

    def slot_of(a, h):
        return owner(-a) * heads + column_at(-h)

    def hand(i, m):
        a, h = every[i]
        n = (m - 1) * sources + i
        source = column.at[slot_of(a, h), pl.ds(head_size, 2 * head_size)]
        return send(source, passed.at[m - 1, i], f_out.at[n], f_in.at[n], sharer_at(m))

    def fill(n, chunk):
        keys = slice(n * rows, (n + 1) * rows)
        k_ref[keys, :] = jnp.transpose(chunk[:head_size].astype(f32)).astype(bf16)
        vt_ref[:head_size, keys] = chunk[head_size:]

    for i, (a, h) in enumerate(every):
        if (a, h) != (0, 0):
            deal(a, h).wait_recv()
        for m in range(1, sharers):
            hand(i, m).start()
        fill(i, column[slot_of(a, h), head_size:])

    def give_back(a, h):
        i = a * heads + h
        return send(
            results.at[a, column_at(h)],
            landed.at[place.head * count + mine],
            r_out.at[i], r_in.at[i], device_at(a, h),
        )

    span = sources * rows
    blocks = [(j + 1) % count for j in range(count)]
    for m in range(sharers):
        if m:
            for i in range(sources):
                hand(i, m).wait_recv()
                fill(m * sources + i, passed[m - 1, i])
        keys = slice(m * span, (m + 1) * span)
        for a in blocks:
            queries = jnp.concatenate(
                [column[owner(a) * heads + n, :head_size] for n in range(heads)], axis=1
            )
            scores = dot(k_ref[keys, :], queries)
            total = dot(vt_ref[:, keys], jnp.exp2(scores).astype(bf16))
            if m:
                total = acc[a] + total
            if m < sharers - 1:
                acc[a] = total
                continue
            result = (total[:head_size] / total[head_size : head_size + 1]).astype(bf16)
            for n in range(heads):
                results[a, n] = result[:, n * rows : (n + 1) * rows]
            for h in range(heads):
                if (a, h) != (0, 0):
                    give_back(a, h).start()
    landed[place.head * count + mine] = results[0, place.head]
    for i in range(2, 5):
        load(i).wait()
    for a, h in every:
        if (a, h) != (0, 0):
            give_back(a, h).wait_recv()
    stream = stream + dot(turned(landed), self_out[...].reshape(-1, depth))
    gather.start(layer_norm(stream).astype(bf16))

    def mlp(k):
        x = gather.rows[pl.ds(place.pair_at(k) * 2, 2)].reshape(-1, depth)
        hidden = jax.nn.gelu(dot(x, win[...]), approximate=True).astype(bf16)
        scatter.give(k, dot(hidden, down[...]))

    gather.near_arrival(0).wait_recv()
    mlp(0)
    gather.forward()
    for k in range(1, place.pairs):
        gather.near_arrival(k).wait_recv()
    for k in range(1, place.pairs):
        mlp(k)
    for k in range(1, place.pairs):
        scatter.relay(k)
    out_ref[...] = (stream + scatter.finish()).astype(bf16)
    scatter.drain()
    gather.drain()
    for h in range(1, heads):
        swap(h).wait_send()
    for a, h in every:
        if (a, h) != (0, 0):
            deal(a, h).wait_send()
            give_back(a, h).wait_send()
    for i in range(sources):
        for m in range(1, sharers):
            hand(i, m).wait_send()


def late_stage(tri, mixed, cross_out, qkv, self_out, win, wdown, toks, heads, head_size, factor):
    rows, depth = tri.shape
    width = mixed.shape[1]
    count = width // head_size
    sharers = toks // count
    sources = count * heads
    vmem = pl.BlockSpec(memory_space=pltpu.VMEM)
    anywhere = pl.BlockSpec(memory_space=pl.ANY)
    dma = pltpu.SemaphoreType.DMA
    passes = max(1, sources * (sharers - 1))
    return pl.pallas_call(
        functools.partial(
            late_kernel, toks=toks, heads=heads, head_size=head_size, factor=factor
        ),
        out_shape=jax.ShapeDtypeStruct((rows, depth), bf16),
        in_specs=[vmem] * 2 + [anywhere] * 5,
        out_specs=vmem,
        scratch_shapes=[
            pltpu.VMEM(cross_out.shape, bf16),
            pltpu.VMEM(qkv.shape, bf16),
            pltpu.VMEM(self_out.shape, bf16),
            pltpu.VMEM(win.shape, bf16),
            pltpu.VMEM(wdown.shape, bf16),
            pltpu.VMEM((heads, width, rows), bf16),
            pltpu.VMEM((heads, count, 3 * head_size, rows), bf16),
            pltpu.VMEM((sources, 3 * head_size, rows), bf16),
            pltpu.VMEM((max(1, sharers - 1), sources, 2 * head_size, rows), bf16),
            pltpu.VMEM((toks * heads * rows, head_size), bf16),
            pltpu.VMEM((head_size + ONES, toks * heads * rows), bf16),
            pltpu.VMEM((count, head_size + ONES, heads * rows), f32),
            pltpu.VMEM((count, heads, head_size, rows), bf16),
            pltpu.VMEM((sources, head_size, rows), bf16),
            dma((5,)), dma((heads,)), dma((heads,)),
            dma((sources,)), dma((sources,)),
            dma((passes,)), dma((passes,)),
            dma((sources,)), dma((sources,)),
        ] + Scatter.scratch(heads, rows, depth) + Gather.scratch(heads, rows, depth),
        compiler_params=pltpu.CompilerParams(
            vmem_limit_bytes=VMEM_LIMIT, collective_id=3, has_side_effects=True
        ),
        name="late_stage",
    )(tri, mixed, cross_out, qkv, self_out, win, wdown)


def per_device(
    tri_tokens, image_tokens, cross_q, cross_kv, cross_out, self_qkv, self_out, mlp_in, mlp_out,
    *, tok, head
):
    rows, depth = tri_tokens.shape
    head_size = depth // HEADS
    factor = score_gain / math.sqrt(head_size) * math.log2(math.e)
    width = cross_q.shape[1]
    weights = []
    if rows % 128 == 0:
        weights = [
            cross_out.reshape(2, -1, depth),
            self_qkv.reshape(6, -1, width),
            self_out.reshape(2, -1, depth),
        ]
    mixed, *weights = cross(
        tri_tokens, image_tokens, cross_q, cross_kv, weights, tok, head, head_size, factor
    )
    if weights:
        weights[1] = weights[1].reshape(head, 3, depth, width)
        return late_stage(
            tri_tokens, mixed, *weights, mlp_in, mlp_out, tok, head, head_size, factor
        )
    mixed = mixed.transpose(1, 0, 2).reshape(mixed.shape[1], -1)
    stream, mixed = self_stage(
        tri_tokens, mixed, cross_out, self_qkv, tok, head, head_size, factor
    )
    return mlp_stage(stream, mixed, self_out, mlp_in, mlp_out, tok, head)


def solution(mesh):
    return jax.shard_map(
        functools.partial(per_device, tok=mesh.shape["tok"], head=mesh.shape["head"]),
        mesh=mesh,
        in_specs=(
            P(("tok", "head"), None),
            P("tok", None),
            P(None, "head"),
            P(None, None, "head"),
            P("head", None),
            P(None, None, "head"),
            P("head", None),
            P(None, "head"),
            P("head", None),
        ),
        out_specs=P(("tok", "head"), None),
        check_vma=False,
    )
```

```python
import functools
import math

import jax
import jax.numpy as jnp
from jax import lax
from jax.experimental import pallas as pl
from jax.experimental.pallas import tpu as pltpu
from jax.sharding import PartitionSpec as P

HEADS = 16
score_gain = 2.5
VMEM_LIMIT = 60 << 20
MESH = pl.DeviceIdType.MESH
ONES = 16
FORWARD_AT = 2
QUERY_AT = 3
LAG = 2
STEP = 512
bf16 = jnp.bfloat16
f32 = jnp.float32


def layer_norm(values):
    centered = values - jnp.mean(values, axis=-1, keepdims=True)
    return centered * lax.rsqrt(jnp.mean(centered * centered, axis=-1, keepdims=True) + 1e-05)


def dot(a, b):
    return jnp.dot(a, b, preferred_element_type=f32)


def head_scale(product, head_size):
    width = product.shape[1]
    rows = lax.broadcasted_iota(jnp.int32, (width, width), 0) // head_size
    cols = lax.broadcasted_iota(jnp.int32, (width, width), 1) // head_size
    same = (rows == cols).astype(f32).astype(bf16)
    squares = product * product
    high = squares.astype(bf16)
    low = (squares - high.astype(f32)).astype(bf16)
    total = dot(high, same) + dot(low, same)
    return lax.rsqrt(total * (1.0 / head_size) + 1e-06)


def head_norm_rows(product, head_size, factor):
    width, count = product.shape
    shaped = product.reshape(width // head_size, head_size, count)
    mean = jnp.sum(shaped * shaped, axis=1, keepdims=True) * (1.0 / head_size)
    return (shaped * (lax.rsqrt(mean + 1e-06) * factor)).reshape(width, count)


def send(source, target, send_sem, recv_sem, device):
    copy = pltpu.make_async_remote_copy(
        src_ref=source,
        dst_ref=target,
        send_sem=send_sem,
        recv_sem=recv_sem,
        device_id=device,
        device_id_type=MESH,
    )
    return copy


def greet(devices):
    barrier = pltpu.get_barrier_semaphore()
    for device in devices:
        pl.semaphore_signal(barrier, inc=1, device_id=device, device_id_type=MESH)
    pl.semaphore_wait(barrier, len(devices))


class Place:
    def __init__(self, toks, heads):
        self.toks, self.heads = toks, heads
        self.tok, self.head = lax.axis_index("tok"), lax.axis_index("head")
        self.pairs = heads // 2
        self.pair, self.core = lax.div(self.head, 2), lax.rem(self.head, 2)

    def partner(self):
        return (self.tok, self.pair * 2 + 1 - self.core)

    def pair_at(self, k):
        return lax.rem(self.pair + k + self.pairs, self.pairs)

    def across(self, k):
        return (self.tok, self.pair_at(k) * 2 + self.core)

    def head_peers(self):
        return [self.partner()] + [self.across(k) for k in range(1, self.pairs)]


class Gather:
    @staticmethod
    def scratch(heads, rows, depth):
        dma = pltpu.SemaphoreType.DMA((heads // 2,))
        return [pltpu.VMEM((heads, rows, depth), bf16), dma, dma, dma, dma]

    def __init__(self, place, refs):
        self.place = place
        self.rows, self.pair_out, self.pair_in, self.far_out, self.far_in = refs

    def far(self, k):
        p = self.place
        mine = self.rows.at[p.head]
        return send(mine, mine, self.far_out.at[k], self.far_in.at[k], p.across(k))

    def far_arrival(self, k):
        p = self.place
        slot = self.rows.at[p.pair_at(-k) * 2 + p.core]
        return send(slot, slot, self.far_out.at[k], self.far_in.at[k], p.across(-k))

    def near(self, k):
        p = self.place
        slot = self.rows.at[p.pair_at(-k) * 2 + p.core]
        return send(slot, slot, self.pair_out.at[k], self.pair_in.at[k], p.partner())

    def near_arrival(self, k):
        p = self.place
        slot = self.rows.at[p.pair_at(-k) * 2 + 1 - p.core]
        return send(slot, slot, self.pair_out.at[k], self.pair_in.at[k], p.partner())

    def start(self, value):
        self.rows[self.place.head] = value
        for k in range(1, self.place.pairs):
            self.far(k).start()
        self.near(0).start()

    def forward(self):
        for k in range(1, self.place.pairs):
            self.far_arrival(k).wait_recv()
            self.near(k).start()

    def finish(self):
        for k in range(self.place.pairs):
            self.near_arrival(k).wait_recv()

    def drain(self):
        for k in range(1, self.place.pairs):
            self.far(k).wait_send()
        for k in range(self.place.pairs):
            self.near(k).wait_send()


def join(tiles, width):
    total = functools.reduce(lambda a, b: a + b, [t.astype(f32) for t in tiles])
    return total[:width], total[width : width + 8] + total[width + 8 : width + 16]


def pack(mixed, totals):
    high = totals.astype(bf16).astype(f32)
    return jnp.concatenate([mixed, high, totals - high], axis=0).astype(bf16)


def attend_block(queries, k_ref, vt_ref, head_size):
    width, count = queries.shape
    lanes = min(128, width)
    keys = k_ref.shape[0]
    block = math.gcd(keys, 2048)
    row = lax.broadcasted_iota(jnp.int32, (lanes, count), 0) // head_size
    place = lax.broadcasted_iota(jnp.int32, (ONES, count), 0) % 8
    mixed, totals = [], jnp.zeros((ONES, count), f32)
    for h in range(width // head_size):
        first = h * head_size // lanes * lanes
        picked = queries[first : first + lanes]
        if lanes > head_size:
            picked = jnp.where(row == h % (lanes // head_size), picked, jnp.zeros_like(picked))
        acc = jnp.zeros((head_size + ONES, count), f32)
        for i in range(keys // block):
            rows = slice(i * block, (i + 1) * block)
            scores = dot(k_ref[rows, first : first + lanes], picked)
            acc = acc + dot(vt_ref[h, :, rows], jnp.exp2(scores).astype(bf16))
        mixed.append(acc[:head_size])
        totals = jnp.where(place == h, acc[head_size:], totals)
    return pack(jnp.concatenate(mixed, axis=0), totals[:8])


class Share:
    @staticmethod
    def scratch(count, heads):
        dma = pltpu.SemaphoreType.DMA((count * (heads // 2),))
        return [dma, dma, dma, dma, pltpu.SemaphoreType.DMA((count,))]

    def __init__(self, place, own, full, sems):
        self.place, self.own, self.full = place, own, full
        self.far_out, self.far_in, self.near_out, self.near_in, self.local_sem = sems

    def far(self, i, k):
        p = self.place
        n = i * p.pairs + k
        return send(
            self.own[i], self.full[i](p.head), self.far_out.at[n], self.far_in.at[n], p.across(k)
        )

    def near(self, i, k):
        p = self.place
        n = i * p.pairs + k
        slot = self.full[i](p.pair_at(-k) * 2 + p.core)
        source = slot if k else self.own[i]
        return send(source, slot, self.near_out.at[n], self.near_in.at[n], p.partner())

    def local(self, i):
        return pltpu.make_async_copy(
            self.own[i], self.full[i](self.place.head), self.local_sem.at[i]
        )

    def start(self, i):
        for k in range(1, self.place.pairs):
            self.far(i, k).start()
        self.near(i, 0).start()
        self.local(i).start()

    def forward(self, i):
        for k in range(1, self.place.pairs):
            self.far(i, k).wait_recv()
            self.near(i, k).start()

    def finish(self, i):
        self.local(i).wait()
        for k in range(self.place.pairs):
            self.near(i, k).wait()
        for k in range(1, self.place.pairs):
            self.far(i, k).wait_send()


def pick(step, values):
    chosen = jnp.int32(values[0])
    for i, value in enumerate(values):
        chosen = jnp.where(step == i, jnp.int32(value), chosen)
    return chosen


def block_order(lines):
    order = sorted(range(1, lines), key=lambda k: (-min(k, lines - k), k))
    turns = [(False, lines)]
    for k in order[:-1]:
        turns += [(True, k), (False, k)]
    for k in order[-1:]:
        turns += [(False, k), (True, k)]
    turns.append((True, lines))
    take, combine = {}, {}
    for j, k in enumerate(order):
        early = j + 1 if j < 3 else 2 * j - 1
        take.setdefault(min(early, min(turns.index((m, k)) for m in (True, False))), []).append(k)
        last = j == len(order) - 1
        after = turns.index((True, k)) if last else turns.index((False, k)) + LAG
        combine.setdefault(min(after, len(turns) - (2 if last else 3)), []).append(k)
    return order, turns, take, combine


def cross_kernel(
    tri_ref, image_ref, wq_ref, wkv_ref, *rest,
    toks, heads, head_size, factor, shared,
):
    own_refs, out_ref, full_refs = rest[:shared], rest[shared], rest[shared + 1 : 2 * shared + 1]
    cross_body(
        tri_ref, image_ref, wq_ref, wkv_ref, own_refs, out_ref, full_refs,
        *rest[2 * shared + 1 :], toks=toks, heads=heads, head_size=head_size, factor=factor,
    )


def cross_body(
    tri_ref, image_ref, wq_ref, wkv_ref, own_refs, out_ref, full_refs,
    image, k_ref, vt_ref, queries, tiles, pair_tiles, joined, far_tiles,
    image_sem, q_out, q_in, f_out, f_in, p_out, p_in, c_out, c_in, *refs,
    toks, heads, head_size, factor,
):
    place = Place(toks, heads)
    _, width, rows_each = out_ref.shape
    group = rows_each * heads
    lines = toks // 2
    order, turns, take, combine = block_order(lines)
    line, side = lax.div(place.tok, 2), lax.rem(place.tok, 2)
    neighbour = (line * 2 + 1 - side, place.head)

    def line_at(k):
        return lax.rem(line + k + lines, lines)

    def peer(k):
        return (line_at(k) * 2 + side, place.head)

    keys = k_ref.shape[0]
    step_rows = math.gcd(keys, STEP)
    steps = keys // step_rows

    def fetch(i):
        rows = pl.ds(pl.multiple_of(i * step_rows, step_rows), step_rows)
        return pltpu.make_async_copy(image_ref.at[rows], image.at[rows], image_sem.at[i])

    for i in range(steps):
        fetch(i).start()
    greet(place.head_peers() + [neighbour] + [peer(k) for k in range(1, lines)])
    gather = Gather(place, refs[:5])
    own, full = [], []
    for mine, whole in zip(own_refs, full_refs):
        for j in range(mine.shape[0]):
            own.append(mine.at[j])
            full.append(functools.partial(lambda slot, whole, j: whole.at[slot, j], whole=whole, j=j))
    share = Share(place, own, full, refs[5:]) if own else None
    gather.start(layer_norm(tri_ref[...].astype(f32)).astype(bf16))
    vt_ref[:, head_size:, :] = jnp.ones((width // head_size, ONES, keys), bf16)

    def q_send(k):
        mine = queries.at[place.tok]
        return send(mine, mine, q_out.at[k], q_in.at[k], peer(-k) if k else neighbour)

    def q_arrival(k):
        slot = queries.at[line_at(k) * 2 + side]
        return send(slot, slot, q_out.at[k], q_in.at[k], peer(k))

    def project(i, carry):
        @pl.when(i == FORWARD_AT * steps // 8)
        def _():
            gather.forward()

        @pl.when(i == QUERY_AT * steps // 8)
        def _():
            gather.finish()
            x = gather.rows[...].reshape(group, -1)
            product = jnp.transpose(dot(x, wq_ref[...]))
            queries[place.tok] = head_norm_rows(product, head_size, factor).astype(bf16)
            q_send(0).start()
            for k in order[:1]:
                q_send(k).start()
            for n in range(min(2, len(own))):
                share.start(n)

        rows = pl.ds(pl.multiple_of(i * step_rows, step_rows), step_rows)
        fetch(i).wait()
        x = image[rows, :]
        k = dot(x, wkv_ref[0])
        k_ref[rows, :] = (k * head_scale(k, head_size)).astype(bf16)
        v = jnp.transpose(dot(x, wkv_ref[1])).astype(bf16)
        vt_ref[:, :head_size, rows] = v.reshape(width // head_size, head_size, step_rows)
        return carry

    lax.fori_loop(0, steps, project, 0)
    def forward(k, slot):
        block = queries.at[slot]
        return send(block, block, f_out.at[k], f_in.at[k], neighbour)

    def pair_send(k, s):
        return send(tiles.at[s], pair_tiles.at[k], p_out.at[k], p_in.at[k], neighbour)

    def far_send(k):
        return send(joined.at[k], far_tiles.at[k], c_out.at[k], c_in.at[k], peer(k))

    def turn_of(n):
        return min(len(turns) - 2, max(0, n - 3))

    def arrive(k):
        slot = lax.rem(line + k, lines) * 2 + side
        block = queries.at[slot]
        send(block, block, q_out.at[k], q_in.at[k], neighbour).wait_recv()
        forward(k, slot).start()

    def before(i):
        mine, k = turns[i]
        if not mine and k == lines:
            block = queries.at[line * 2 + 1 - side]
            send(block, block, q_out.at[0], q_in.at[0], neighbour).wait_recv()
        for j, later in enumerate(order):
            if j and i == max(0, 2 * j - 4):
                q_send(later).start()
        for taken in take.get(i, []):
            arrive(taken)
        if not mine and k < lines:
            forward(k, lax.rem(line + k, lines) * 2 + 1 - side).wait_recv()
        if own:
            for n in range(2, len(own)):
                if i == turn_of(n):
                    share.start(n)

    def after(i):
        mine, k = turns[i]
        if not mine and k < lines:
            pair_send(k, i).start()
        if i == min(1, len(turns) - 2):
            pair_send(lines, 0).start()
        for done in combine.get(i, []):
            pair_send(done, i).wait_recv()
            joined[done] = pack(
                *join([tiles[turns.index((True, done))], pair_tiles[done]], width)
            )
            far_send(done).start()
        if own:
            for n in range(len(own)):
                if i == min(len(turns) - 1, turn_of(n) + 1):
                    share.forward(n)

    def attend(s, carry):
        for i in range(len(turns)):
            pl.when(s == i)(functools.partial(before, i))
        k = pick(s, [k for _, k in turns])
        mine = pick(s, [int(m) for m, _ in turns])
        slot = lax.rem(line + k, lines) * 2 + mine * side + (1 - mine) * (1 - side)
        tiles[s] = attend_block(queries[slot], k_ref, vt_ref, head_size)
        for i in range(len(turns)):
            pl.when(s == i)(functools.partial(after, i))
        return carry

    lax.fori_loop(0, len(turns), attend, 0)
    pair_send(lines, 0).wait_recv()
    for k in range(1, lines):
        far_send(k).wait_recv()
    mixed, totals = join(
        [tiles[2 * lines - 1], pair_tiles[lines]] + [far_tiles[k] for k in range(1, lines)], width
    )
    for h in range(width // head_size):
        rows = slice(h * head_size, (h + 1) * head_size)
        mix = (mixed[rows] / totals[h : h + 1]).astype(bf16)
        for n in range(heads):
            out_ref[n, rows, :] = mix[:, n * rows_each : (n + 1) * rows_each]
    gather.drain()
    for k in range(lines):
        q_send(k).wait_send()
    for k in range(1, lines):
        forward(k, 0).wait_send()
        far_send(k).wait_send()
    for k in range(1, lines + 1):
        pair_send(k, 0).wait_send()
    for n in range(len(own)):
        share.finish(n)


def cross(tri, image, wq, wkv, weights, toks, heads, head_size, factor):
    rows, depth = tri.shape
    keys = image.shape[0]
    width = wq.shape[1]
    group = rows * heads
    lines = toks // 2
    tile = (width + 16, group)
    vmem = pl.BlockSpec(memory_space=pltpu.VMEM)
    anywhere = pl.BlockSpec(memory_space=pl.ANY)
    pieces = sum(w.shape[0] for w in weights)
    dma = pltpu.SemaphoreType.DMA
    return pl.pallas_call(
        functools.partial(
            cross_kernel, toks=toks, heads=heads, head_size=head_size, factor=factor,
            shared=len(weights),
        ),
        out_shape=[jax.ShapeDtypeStruct((heads, width, rows), bf16)]
        + [jax.ShapeDtypeStruct((heads,) + w.shape, bf16) for w in weights],
        in_specs=[vmem, anywhere, vmem, vmem] + [anywhere] * len(weights),
        out_specs=[vmem] + [anywhere] * len(weights),
        scratch_shapes=[
            pltpu.VMEM((keys, depth), bf16),
            pltpu.VMEM((keys, width), bf16),
            pltpu.VMEM((width // head_size, head_size + ONES, keys), bf16),
            pltpu.VMEM((toks, width, group), bf16),
            pltpu.VMEM((2 * lines,) + tile, bf16),
            pltpu.VMEM((lines + 1,) + tile, bf16),
            pltpu.VMEM((lines,) + tile, bf16),
            pltpu.VMEM((lines,) + tile, bf16),
            dma((keys // math.gcd(keys, STEP),)),
            dma((lines,)), dma((lines,)),
            dma((lines,)), dma((lines,)),
            dma((lines + 1,)), dma((lines + 1,)),
            dma((lines,)), dma((lines,)),
        ]
        + Gather.scratch(heads, rows, depth)
        + (Share.scratch(pieces, heads) if weights else []),
        compiler_params=pltpu.CompilerParams(
            vmem_limit_bytes=VMEM_LIMIT, collective_id=0, has_side_effects=True
        ),
        name="cross",
    )(tri, image, wq, wkv, *weights)


class Scatter:
    @staticmethod
    def scratch(heads, rows, depth):
        pairs = heads // 2
        dma = pltpu.SemaphoreType.DMA((pairs,))
        tiles = [pltpu.VMEM((pairs, rows, depth), bf16)] * 3
        return [pltpu.VMEM((pairs, 2, rows, depth), bf16)] + tiles + [dma] * 4

    def __init__(self, place, refs):
        self.place = place
        self.part, self.close, self.sums, self.distant = refs[:4]
        self.near_out, self.near_in, self.far_out, self.far_in = refs[4:]

    def near(self, k):
        p = self.place
        return send(
            self.part.at[k, 1 - p.core],
            self.close.at[k],
            self.near_out.at[k],
            self.near_in.at[k],
            p.partner(),
        )

    def far(self, k):
        return send(
            self.sums.at[k],
            self.distant.at[k],
            self.far_out.at[k],
            self.far_in.at[k],
            self.place.across(k),
        )

    def give(self, k, value):
        self.part[k] = value.reshape(self.part.shape[1:]).astype(bf16)
        self.near(k).start()

    def near_sum(self, k):
        self.near(k).wait_recv()
        return self.part[k, self.place.core].astype(f32) + self.close[k].astype(f32)

    def relay(self, k):
        self.sums[k] = self.near_sum(k).astype(bf16)
        self.far(k).start()

    def finish(self):
        total = self.near_sum(0)
        for k in range(1, self.place.pairs):
            self.far(k).wait_recv()
            total = total + self.distant[k].astype(f32)
        return total

    def drain(self):
        for k in range(self.place.pairs):
            self.near(k).wait_send()
        for k in range(1, self.place.pairs):
            self.far(k).wait_send()


def collect(place, scatter, mix, weight_ref):
    both = mix.shape[0] // place.pairs

    def partial(k):
        rows = pl.ds(pl.multiple_of(place.pair_at(k) * both, both), both)
        return dot(mix[rows, :], weight_ref[...])

    for k in range(1, place.pairs):
        scatter.give(k, partial(k))
    scatter.give(0, partial(0))
    for k in range(1, place.pairs):
        scatter.relay(k)
    return scatter.finish()


def self_kernel(
    tri_ref, mixed_ref, wout_ref, wqkv_ref, stream_ref, out_ref,
    mix, chunks, column, passed, k_ref, vt_ref, acc, results, landed,
    a_out, a_in, f_out, f_in, o_out, o_in, *refs,
    toks, heads, head_size, factor,
):
    place = Place(toks, heads)
    width, group = out_ref.shape
    count = width // head_size
    sharers = toks // count
    mine, part = lax.div(place.tok, sharers), lax.rem(place.tok, sharers)

    def owner(k):
        return lax.rem(mine + k + count, count)

    def owner_at(k):
        return (owner(k) * sharers + part, place.head)

    def sharer_at(m):
        return (mine * sharers + lax.rem(part + m, sharers), place.head)

    greet(
        place.head_peers()
        + [owner_at(k) for k in range(1, count)]
        + [sharer_at(m) for m in range(1, sharers)]
    )
    scatter = Scatter(place, refs[:8])
    gather = Gather(place, refs[8:])
    mix[...] = jnp.transpose(mixed_ref[...].astype(f32)).astype(bf16)
    vt_ref[head_size:, :] = jnp.ones((ONES, vt_ref.shape[1]), bf16)
    stream = tri_ref[...].astype(f32) + collect(place, scatter, mix, wout_ref)
    stream_ref[...] = stream
    gather.start(layer_norm(stream).astype(bf16))
    gather.forward()
    gather.finish()
    x = gather.rows[...].reshape(group, -1)
    for j in range(3):
        product = jnp.transpose(dot(x, wqkv_ref[j]))
        if j < 2:
            product = head_norm_rows(product, head_size, 1.0 if j else factor)
        chunks[:, j * head_size : (j + 1) * head_size, :] = product.reshape(
            count, head_size, group
        ).astype(bf16)

    def deal(k):
        return send(
            chunks.at[owner(k)], column.at[mine], a_out.at[k], a_in.at[k], owner_at(k)
        )

    def hand(k, m):
        source = column.at[owner(-k), pl.ds(head_size, 2 * head_size)]
        i = k * (sharers - 1) + m - 1
        return send(source, passed.at[k, m - 1], f_out.at[i], f_in.at[i], sharer_at(m))

    def fill(n, chunk):
        rows = slice(n * group, (n + 1) * group)
        k_ref[rows, :] = jnp.transpose(chunk[:head_size].astype(f32)).astype(bf16)
        vt_ref[:head_size, rows] = chunk[head_size:]

    for k in range(1, count):
        deal(k).start()
    column[mine] = chunks[mine]
    for k in range(count):
        if k:
            deal(k).wait_recv()
        for m in range(1, sharers):
            hand(k, m).start()
        fill(k, column[owner(-k), head_size:])

    def give_back(j):
        return send(results.at[j], landed.at[mine], o_out.at[j], o_in.at[j], owner_at(j + 1))

    span = count * group
    for m in range(sharers):
        if m:
            for k in range(count):
                hand(k, m).wait_recv()
                fill(m * count + k, passed[k, m - 1])
        keys = slice(m * span, (m + 1) * span)
        for j in range(count):
            scores = dot(k_ref[keys, :], column[owner(j + 1), :head_size])
            total = dot(vt_ref[:, keys], jnp.exp2(scores).astype(bf16))
            if m:
                total = acc[j] + total
            if m < sharers - 1:
                acc[j] = total
                continue
            result = (total[:head_size] / total[head_size : head_size + 1]).astype(bf16)
            if j == count - 1:
                landed[mine] = result
            else:
                results[j] = result
                give_back(j).start()
    for j in range(count - 1):
        give_back(j).wait_recv()
    out_ref[...] = landed[...].reshape(width, group)
    scatter.drain()
    gather.drain()
    for k in range(1, count):
        deal(k).wait_send()
    for k in range(count):
        for m in range(1, sharers):
            hand(k, m).wait_send()
    for j in range(count - 1):
        give_back(j).wait_send()


def self_stage(tri, mixed, wout, wqkv, toks, heads, head_size, factor):
    rows, depth = tri.shape
    width, group = mixed.shape
    count = width // head_size
    sharers = toks // count
    vmem = pl.BlockSpec(memory_space=pltpu.VMEM)
    dma = pltpu.SemaphoreType.DMA
    passes = max(1, count * (sharers - 1))
    return pl.pallas_call(
        functools.partial(
            self_kernel, toks=toks, heads=heads, head_size=head_size, factor=factor
        ),
        out_shape=[
            jax.ShapeDtypeStruct((rows, depth), f32),
            jax.ShapeDtypeStruct((width, group), bf16),
        ],
        in_specs=[vmem] * 4,
        out_specs=[vmem] * 2,
        scratch_shapes=[
            pltpu.VMEM((group, width), bf16),
            pltpu.VMEM((count, 3 * head_size, group), bf16),
            pltpu.VMEM((count, 3 * head_size, group), bf16),
            pltpu.VMEM((count, max(1, sharers - 1), 2 * head_size, group), bf16),
            pltpu.VMEM((toks * group, head_size), bf16),
            pltpu.VMEM((head_size + ONES, toks * group), bf16),
            pltpu.VMEM((count, head_size + ONES, group), f32),
            pltpu.VMEM((count, head_size, group), bf16),
            pltpu.VMEM((count, head_size, group), bf16),
            dma((count,)), dma((count,)),
            dma((passes,)), dma((passes,)),
            dma((count,)), dma((count,)),
        ] + Scatter.scratch(heads, rows, depth) + Gather.scratch(heads, rows, depth),
        compiler_params=pltpu.CompilerParams(
            vmem_limit_bytes=VMEM_LIMIT, collective_id=1, has_side_effects=True
        ),
        name="self_stage",
    )(tri, mixed, wout, wqkv)


def mlp_kernel(
    stream_ref, mixed_ref, wout_ref, win_ref, wdown_ref, out_ref, mix, *refs, toks, heads
):
    place = Place(toks, heads)
    greet(place.head_peers())
    scatter = Scatter(place, refs[:8])
    second = Scatter(place, refs[8:16])
    gather = Gather(place, refs[16:])
    mix[...] = jnp.transpose(mixed_ref[...].astype(f32)).astype(bf16)
    stream = stream_ref[...] + collect(place, scatter, mix, wout_ref)
    gather.start(layer_norm(stream).astype(bf16))

    def mlp(k):
        x = gather.rows[pl.ds(place.pair_at(k) * 2, 2)].reshape(-1, stream.shape[1])
        hidden = jax.nn.gelu(dot(x, win_ref[...]), approximate=True).astype(bf16)
        second.give(k, dot(hidden, wdown_ref[...]))

    gather.near_arrival(0).wait_recv()
    mlp(0)
    gather.forward()
    for k in range(1, place.pairs):
        gather.near_arrival(k).wait_recv()
    for k in range(1, place.pairs):
        mlp(k)
    for k in range(1, place.pairs):
        second.relay(k)
    out_ref[...] = (stream + second.finish()).astype(bf16)
    scatter.drain()
    second.drain()
    gather.drain()


def mlp_stage(stream, mixed, wout, win, wdown, toks, heads):
    rows, depth = stream.shape
    width, group = mixed.shape
    vmem = pl.BlockSpec(memory_space=pltpu.VMEM)
    return pl.pallas_call(
        functools.partial(mlp_kernel, toks=toks, heads=heads),
        out_shape=jax.ShapeDtypeStruct((rows, depth), bf16),
        in_specs=[vmem] * 5,
        out_specs=vmem,
        scratch_shapes=[pltpu.VMEM((group, width), bf16)]
        + Scatter.scratch(heads, rows, depth) * 2
        + Gather.scratch(heads, rows, depth),
        compiler_params=pltpu.CompilerParams(
            vmem_limit_bytes=VMEM_LIMIT, collective_id=2, has_side_effects=True
        ),
        name="mlp_stage",
    )(stream, mixed, wout, win, wdown)


def late_kernel(
    tri_ref, mixed_ref, cross_out_ref, qkv_ref, self_out_ref, win_ref, wdown_ref, out_ref,
    cross_out, qkv, self_out, win, down, mixes, chunks, column, passed, k_ref, vt_ref, acc,
    results, landed, load_sem, m_out, m_in, a_out, a_in, f_out, f_in, r_out, r_in, *refs,
    toks, heads, head_size, factor,
):
    place = Place(toks, heads)
    rows, depth = tri_ref.shape
    width = mixed_ref.shape[1]
    count = width // head_size
    sharers = toks // count
    sources = count * heads
    mine, part = lax.div(place.tok, sharers), lax.rem(place.tok, sharers)
    every = [(a, h) for h in range(heads) for a in range(count)]

    def owner(a):
        return lax.rem(mine + a + count, count)

    def column_at(h):
        return lax.rem(place.head + h + heads, heads)

    def device_at(a, h):
        return (owner(a) * sharers + part, column_at(h))

    def sharer_at(m):
        return (mine * sharers + lax.rem(part + m, sharers), place.head)

    def load(i):
        source, target = [
            (cross_out_ref, cross_out), (qkv_ref, qkv), (self_out_ref, self_out),
            (win_ref, win), (wdown_ref, down),
        ][i]
        return pltpu.make_async_copy(source, target, load_sem.at[i])

    for i in range(5):
        load(i).start()
    greet(
        [device_at(a, h) for a, h in every if (a, h) != (0, 0)]
        + [sharer_at(m) for m in range(1, sharers)]
    )
    scatter = Scatter(place, refs[:8])
    gather = Gather(place, refs[8:])

    def swap(h):
        return send(
            mixed_ref.at[column_at(h)], mixes.at[place.head], m_out.at[h], m_in.at[h],
            device_at(0, h),
        )

    for h in range(1, heads):
        swap(h).start()
    mixes[place.head] = mixed_ref[place.head]
    vt_ref[head_size:, :] = jnp.ones((ONES, vt_ref.shape[1]), bf16)
    load(0).wait()
    for h in range(1, heads):
        swap(h).wait_recv()

    def turned(ref):
        return jnp.transpose(ref[...].reshape(-1, rows).astype(f32)).astype(bf16)

    stream = tri_ref[...].astype(f32) + dot(turned(mixes), cross_out[...].reshape(-1, depth))
    x = layer_norm(stream).astype(bf16)
    load(1).wait()

    def deal(a, h):
        i = a * heads + h
        return send(
            chunks.at[column_at(h), owner(a)],
            column.at[mine * heads + place.head],
            a_out.at[i], a_in.at[i], device_at(a, h),
        )

    def project(h):
        n = column_at(h)
        for j in range(3):
            product = jnp.transpose(dot(x, qkv[n, j]))
            if j < 2:
                product = head_norm_rows(product, head_size, 1.0 if j else factor)
            chunks[n, :, j * head_size : (j + 1) * head_size, :] = product.reshape(
                count, head_size, rows
            ).astype(bf16)

    for h in range(heads):
        project(h)
        for a in sorted(range(count), key=lambda a: -min(a, count - a)):
            if (a, h) != (0, 0):
                deal(a, h).start()
    column[mine * heads + place.head] = chunks[place.head, mine]

    def slot_of(a, h):
        return owner(-a) * heads + column_at(-h)

    def hand(i, m):
        a, h = every[i]
        n = (m - 1) * sources + i
        source = column.at[slot_of(a, h), pl.ds(head_size, 2 * head_size)]
        return send(source, passed.at[m - 1, i], f_out.at[n], f_in.at[n], sharer_at(m))

    def fill(n, chunk):
        keys = slice(n * rows, (n + 1) * rows)
        k_ref[keys, :] = jnp.transpose(chunk[:head_size].astype(f32)).astype(bf16)
        vt_ref[:head_size, keys] = chunk[head_size:]

    for i, (a, h) in enumerate(every):
        if (a, h) != (0, 0):
            deal(a, h).wait_recv()
        for m in range(1, sharers):
            hand(i, m).start()
        fill(i, column[slot_of(a, h), head_size:])

    def give_back(a, h):
        i = a * heads + h
        return send(
            results.at[a, column_at(h)],
            landed.at[place.head * count + mine],
            r_out.at[i], r_in.at[i], device_at(a, h),
        )

    span = sources * rows
    blocks = [(j + 1) % count for j in range(count)]
    for m in range(sharers):
        if m:
            for i in range(sources):
                hand(i, m).wait_recv()
                fill(m * sources + i, passed[m - 1, i])
        keys = slice(m * span, (m + 1) * span)
        for a in blocks:
            queries = jnp.concatenate(
                [column[owner(a) * heads + n, :head_size] for n in range(heads)], axis=1
            )
            scores = dot(k_ref[keys, :], queries)
            total = dot(vt_ref[:, keys], jnp.exp2(scores).astype(bf16))
            if m:
                total = acc[a] + total
            if m < sharers - 1:
                acc[a] = total
                continue
            result = (total[:head_size] / total[head_size : head_size + 1]).astype(bf16)
            for n in range(heads):
                results[a, n] = result[:, n * rows : (n + 1) * rows]
            for h in range(heads):
                if (a, h) != (0, 0):
                    give_back(a, h).start()
    landed[place.head * count + mine] = results[0, place.head]
    for i in range(2, 5):
        load(i).wait()
    for a, h in every:
        if (a, h) != (0, 0):
            give_back(a, h).wait_recv()
    stream = stream + dot(turned(landed), self_out[...].reshape(-1, depth))
    gather.start(layer_norm(stream).astype(bf16))

    def mlp(k):
        x = gather.rows[pl.ds(place.pair_at(k) * 2, 2)].reshape(-1, depth)
        hidden = jax.nn.gelu(dot(x, win[...]), approximate=True).astype(bf16)
        scatter.give(k, dot(hidden, down[...]))

    gather.near_arrival(0).wait_recv()
    mlp(0)
    gather.forward()
    for k in range(1, place.pairs):
        gather.near_arrival(k).wait_recv()
    for k in range(1, place.pairs):
        mlp(k)
    for k in range(1, place.pairs):
        scatter.relay(k)
    out_ref[...] = (stream + scatter.finish()).astype(bf16)
    scatter.drain()
    gather.drain()
    for h in range(1, heads):
        swap(h).wait_send()
    for a, h in every:
        if (a, h) != (0, 0):
            deal(a, h).wait_send()
            give_back(a, h).wait_send()
    for i in range(sources):
        for m in range(1, sharers):
            hand(i, m).wait_send()


def late_stage(tri, mixed, cross_out, qkv, self_out, win, wdown, toks, heads, head_size, factor):
    rows, depth = tri.shape
    width = mixed.shape[1]
    count = width // head_size
    sharers = toks // count
    sources = count * heads
    vmem = pl.BlockSpec(memory_space=pltpu.VMEM)
    anywhere = pl.BlockSpec(memory_space=pl.ANY)
    dma = pltpu.SemaphoreType.DMA
    passes = max(1, sources * (sharers - 1))
    return pl.pallas_call(
        functools.partial(
            late_kernel, toks=toks, heads=heads, head_size=head_size, factor=factor
        ),
        out_shape=jax.ShapeDtypeStruct((rows, depth), bf16),
        in_specs=[vmem] * 2 + [anywhere] * 5,
        out_specs=vmem,
        scratch_shapes=[
            pltpu.VMEM(cross_out.shape, bf16),
            pltpu.VMEM(qkv.shape, bf16),
            pltpu.VMEM(self_out.shape, bf16),
            pltpu.VMEM(win.shape, bf16),
            pltpu.VMEM(wdown.shape, bf16),
            pltpu.VMEM((heads, width, rows), bf16),
            pltpu.VMEM((heads, count, 3 * head_size, rows), bf16),
            pltpu.VMEM((sources, 3 * head_size, rows), bf16),
            pltpu.VMEM((max(1, sharers - 1), sources, 2 * head_size, rows), bf16),
            pltpu.VMEM((toks * heads * rows, head_size), bf16),
            pltpu.VMEM((head_size + ONES, toks * heads * rows), bf16),
            pltpu.VMEM((count, head_size + ONES, heads * rows), f32),
            pltpu.VMEM((count, heads, head_size, rows), bf16),
            pltpu.VMEM((sources, head_size, rows), bf16),
            dma((5,)), dma((heads,)), dma((heads,)),
            dma((sources,)), dma((sources,)),
            dma((passes,)), dma((passes,)),
            dma((sources,)), dma((sources,)),
        ] + Scatter.scratch(heads, rows, depth) + Gather.scratch(heads, rows, depth),
        compiler_params=pltpu.CompilerParams(
            vmem_limit_bytes=VMEM_LIMIT, collective_id=3, has_side_effects=True
        ),
        name="late_stage",
    )(tri, mixed, cross_out, qkv, self_out, win, wdown)


def per_device(
    tri_tokens, image_tokens, cross_q, cross_kv, cross_out, self_qkv, self_out, mlp_in, mlp_out,
    *, tok, head
):
    rows, depth = tri_tokens.shape
    head_size = depth // HEADS
    factor = score_gain / math.sqrt(head_size) * math.log2(math.e)
    width = cross_q.shape[1]
    weights = []
    if rows % 128 == 0:
        weights = [
            cross_out.reshape(2, -1, depth),
            self_qkv.reshape(6, -1, width),
            self_out.reshape(2, -1, depth),
        ]
    mixed, *weights = cross(
        tri_tokens, image_tokens, cross_q, cross_kv, weights, tok, head, head_size, factor
    )
    if weights:
        weights[1] = weights[1].reshape(head, 3, depth, width)
        return late_stage(
            tri_tokens, mixed, *weights, mlp_in, mlp_out, tok, head, head_size, factor
        )
    mixed = mixed.transpose(1, 0, 2).reshape(mixed.shape[1], -1)
    stream, mixed = self_stage(
        tri_tokens, mixed, cross_out, self_qkv, tok, head, head_size, factor
    )
    return mlp_stage(stream, mixed, self_out, mlp_in, mlp_out, tok, head)


def solution(mesh):
    return jax.shard_map(
        functools.partial(per_device, tok=mesh.shape["tok"], head=mesh.shape["head"]),
        mesh=mesh,
        in_specs=(
            P(("tok", "head"), None),
            P("tok", None),
            P(None, "head"),
            P(None, None, "head"),
            P("head", None),
            P(None, None, "head"),
            P("head", None),
            P(None, "head"),
            P("head", None),
        ),
        out_specs=P(("tok", "head"), None),
        check_vma=False,
    )
```

```python
import functools
import math

import jax
import jax.numpy as jnp
from jax import lax
from jax.experimental import pallas as pl
from jax.experimental.pallas import tpu as pltpu
from jax.sharding import PartitionSpec as P

HEADS = 16
score_gain = 2.5
VMEM_LIMIT = 60 << 20
MESH = pl.DeviceIdType.MESH
ONES = 16
FORWARD_AT = 2
QUERY_AT = 3
LAG = 2
STEP = 512
bf16 = jnp.bfloat16
f32 = jnp.float32


def layer_norm(values):
    centered = values - jnp.mean(values, axis=-1, keepdims=True)
    return centered * lax.rsqrt(jnp.mean(centered * centered, axis=-1, keepdims=True) + 1e-05)


def dot(a, b):
    return jnp.dot(a, b, preferred_element_type=f32)


def head_scale(product, head_size):
    width = product.shape[1]
    rows = lax.broadcasted_iota(jnp.int32, (width, width), 0) // head_size
    cols = lax.broadcasted_iota(jnp.int32, (width, width), 1) // head_size
    same = (rows == cols).astype(f32).astype(bf16)
    squares = product * product
    high = squares.astype(bf16)
    low = (squares - high.astype(f32)).astype(bf16)
    total = dot(high, same) + dot(low, same)
    return lax.rsqrt(total * (1.0 / head_size) + 1e-06)


def head_norm_rows(product, head_size, factor):
    width, count = product.shape
    shaped = product.reshape(width // head_size, head_size, count)
    mean = jnp.sum(shaped * shaped, axis=1, keepdims=True) * (1.0 / head_size)
    return (shaped * (lax.rsqrt(mean + 1e-06) * factor)).reshape(width, count)


def send(source, target, send_sem, recv_sem, device):
    copy = pltpu.make_async_remote_copy(
        src_ref=source,
        dst_ref=target,
        send_sem=send_sem,
        recv_sem=recv_sem,
        device_id=device,
        device_id_type=MESH,
    )
    return copy


def greet(devices):
    barrier = pltpu.get_barrier_semaphore()
    for device in devices:
        pl.semaphore_signal(barrier, inc=1, device_id=device, device_id_type=MESH)
    pl.semaphore_wait(barrier, len(devices))


class Place:
    def __init__(self, toks, heads):
        self.toks, self.heads = toks, heads
        self.tok, self.head = lax.axis_index("tok"), lax.axis_index("head")
        self.pairs = heads // 2
        self.pair, self.core = lax.div(self.head, 2), lax.rem(self.head, 2)

    def partner(self):
        return (self.tok, self.pair * 2 + 1 - self.core)

    def pair_at(self, k):
        return lax.rem(self.pair + k + self.pairs, self.pairs)

    def across(self, k):
        return (self.tok, self.pair_at(k) * 2 + self.core)

    def head_peers(self):
        return [self.partner()] + [self.across(k) for k in range(1, self.pairs)]


class Gather:
    @staticmethod
    def scratch(heads, rows, depth):
        dma = pltpu.SemaphoreType.DMA((heads // 2,))
        return [pltpu.VMEM((heads, rows, depth), bf16), dma, dma, dma, dma]

    def __init__(self, place, refs):
        self.place = place
        self.rows, self.pair_out, self.pair_in, self.far_out, self.far_in = refs

    def far(self, k):
        p = self.place
        mine = self.rows.at[p.head]
        return send(mine, mine, self.far_out.at[k], self.far_in.at[k], p.across(k))

    def far_arrival(self, k):
        p = self.place
        slot = self.rows.at[p.pair_at(-k) * 2 + p.core]
        return send(slot, slot, self.far_out.at[k], self.far_in.at[k], p.across(-k))

    def near(self, k):
        p = self.place
        slot = self.rows.at[p.pair_at(-k) * 2 + p.core]
        return send(slot, slot, self.pair_out.at[k], self.pair_in.at[k], p.partner())

    def near_arrival(self, k):
        p = self.place
        slot = self.rows.at[p.pair_at(-k) * 2 + 1 - p.core]
        return send(slot, slot, self.pair_out.at[k], self.pair_in.at[k], p.partner())

    def start(self, value):
        self.rows[self.place.head] = value
        for k in range(1, self.place.pairs):
            self.far(k).start()
        self.near(0).start()

    def forward(self):
        for k in range(1, self.place.pairs):
            self.far_arrival(k).wait_recv()
            self.near(k).start()

    def finish(self):
        for k in range(self.place.pairs):
            self.near_arrival(k).wait_recv()

    def drain(self):
        for k in range(1, self.place.pairs):
            self.far(k).wait_send()
        for k in range(self.place.pairs):
            self.near(k).wait_send()


def join(tiles, width):
    total = functools.reduce(lambda a, b: a + b, [t.astype(f32) for t in tiles])
    return total[:width], total[width : width + 8] + total[width + 8 : width + 16]


def pack(mixed, totals):
    high = totals.astype(bf16).astype(f32)
    return jnp.concatenate([mixed, high, totals - high], axis=0).astype(bf16)


def attend_block(queries, k_ref, vt_ref, head_size):
    width, count = queries.shape
    lanes = min(128, width)
    keys = k_ref.shape[0]
    block = math.gcd(keys, 2048)
    row = lax.broadcasted_iota(jnp.int32, (lanes, count), 0) // head_size
    place = lax.broadcasted_iota(jnp.int32, (ONES, count), 0) % 8
    mixed, totals = [], jnp.zeros((ONES, count), f32)
    for h in range(width // head_size):
        first = h * head_size // lanes * lanes
        picked = queries[first : first + lanes]
        if lanes > head_size:
            picked = jnp.where(row == h % (lanes // head_size), picked, jnp.zeros_like(picked))
        acc = jnp.zeros((head_size + ONES, count), f32)
        for i in range(keys // block):
            rows = slice(i * block, (i + 1) * block)
            scores = dot(k_ref[rows, first : first + lanes], picked)
            acc = acc + dot(vt_ref[h, :, rows], jnp.exp2(scores).astype(bf16))
        mixed.append(acc[:head_size])
        totals = jnp.where(place == h, acc[head_size:], totals)
    return pack(jnp.concatenate(mixed, axis=0), totals[:8])


class Share:
    @staticmethod
    def scratch(count, heads):
        dma = pltpu.SemaphoreType.DMA((count * (heads // 2),))
        return [dma, dma, dma, dma, pltpu.SemaphoreType.DMA((count,))]

    def __init__(self, place, own, full, sems):
        self.place, self.own, self.full = place, own, full
        self.far_out, self.far_in, self.near_out, self.near_in, self.local_sem = sems

    def far(self, i, k):
        p = self.place
        n = i * p.pairs + k
        return send(
            self.own[i], self.full[i](p.head), self.far_out.at[n], self.far_in.at[n], p.across(k)
        )

    def near(self, i, k):
        p = self.place
        n = i * p.pairs + k
        slot = self.full[i](p.pair_at(-k) * 2 + p.core)
        source = slot if k else self.own[i]
        return send(source, slot, self.near_out.at[n], self.near_in.at[n], p.partner())

    def local(self, i):
        return pltpu.make_async_copy(
            self.own[i], self.full[i](self.place.head), self.local_sem.at[i]
        )

    def start(self, i):
        for k in range(1, self.place.pairs):
            self.far(i, k).start()
        self.near(i, 0).start()
        self.local(i).start()

    def forward(self, i):
        for k in range(1, self.place.pairs):
            self.far(i, k).wait_recv()
            self.near(i, k).start()

    def finish(self, i):
        self.local(i).wait()
        for k in range(self.place.pairs):
            self.near(i, k).wait()
        for k in range(1, self.place.pairs):
            self.far(i, k).wait_send()


def pick(step, values):
    chosen = jnp.int32(values[0])
    for i, value in enumerate(values):
        chosen = jnp.where(step == i, jnp.int32(value), chosen)
    return chosen


def block_order(lines):
    order = sorted(range(1, lines), key=lambda k: (-min(k, lines - k), k))
    turns = [(False, lines)]
    for k in order[:-1]:
        turns += [(True, k), (False, k)]
    for k in order[-1:]:
        turns += [(False, k), (True, k)]
    turns.append((True, lines))
    take, combine = {}, {}
    for j, k in enumerate(order):
        early = j + 1 if j < 3 else 2 * j - 1
        take.setdefault(min(early, min(turns.index((m, k)) for m in (True, False))), []).append(k)
        last = j == len(order) - 1
        after = turns.index((True, k)) if last else turns.index((False, k)) + LAG
        combine.setdefault(min(after, len(turns) - (2 if last else 3)), []).append(k)
    return order, turns, take, combine


def cross_kernel(
    tri_ref, image_ref, wq_ref, wkv_ref, *rest,
    toks, heads, head_size, factor, shared,
):
    own_refs, out_ref, full_refs = rest[:shared], rest[shared], rest[shared + 1 : 2 * shared + 1]
    cross_body(
        tri_ref, image_ref, wq_ref, wkv_ref, own_refs, out_ref, full_refs,
        *rest[2 * shared + 1 :], toks=toks, heads=heads, head_size=head_size, factor=factor,
    )


def cross_body(
    tri_ref, image_ref, wq_ref, wkv_ref, own_refs, out_ref, full_refs,
    image, k_ref, vt_ref, queries, tiles, pair_tiles, joined, far_tiles,
    image_sem, q_out, q_in, f_out, f_in, p_out, p_in, c_out, c_in, *refs,
    toks, heads, head_size, factor,
):
    place = Place(toks, heads)
    _, width, rows_each = out_ref.shape
    group = rows_each * heads
    lines = toks // 2
    order, turns, take, combine = block_order(lines)
    line, side = lax.div(place.tok, 2), lax.rem(place.tok, 2)
    neighbour = (line * 2 + 1 - side, place.head)

    def line_at(k):
        return lax.rem(line + k + lines, lines)

    def peer(k):
        return (line_at(k) * 2 + side, place.head)

    keys = k_ref.shape[0]
    step_rows = math.gcd(keys, STEP)
    steps = keys // step_rows

    def fetch(i):
        rows = pl.ds(pl.multiple_of(i * step_rows, step_rows), step_rows)
        return pltpu.make_async_copy(image_ref.at[rows], image.at[rows], image_sem.at[i])

    for i in range(steps):
        fetch(i).start()
    greet(place.head_peers() + [neighbour] + [peer(k) for k in range(1, lines)])
    gather = Gather(place, refs[:5])
    own, full = [], []
    for mine, whole in zip(own_refs, full_refs):
        for j in range(mine.shape[0]):
            own.append(mine.at[j])
            full.append(functools.partial(lambda slot, whole, j: whole.at[slot, j], whole=whole, j=j))
    share = Share(place, own, full, refs[5:]) if own else None
    gather.start(layer_norm(tri_ref[...].astype(f32)).astype(bf16))
    vt_ref[:, head_size:, :] = jnp.ones((width // head_size, ONES, keys), bf16)

    def q_send(k):
        mine = queries.at[place.tok]
        return send(mine, mine, q_out.at[k], q_in.at[k], peer(-k) if k else neighbour)

    def q_arrival(k):
        slot = queries.at[line_at(k) * 2 + side]
        return send(slot, slot, q_out.at[k], q_in.at[k], peer(k))

    def project(i, carry):
        @pl.when(i == FORWARD_AT * steps // 8)
        def _():
            gather.forward()

        @pl.when(i == QUERY_AT * steps // 8)
        def _():
            gather.finish()
            x = gather.rows[...].reshape(group, -1)
            product = jnp.transpose(dot(x, wq_ref[...]))
            queries[place.tok] = head_norm_rows(product, head_size, factor).astype(bf16)
            q_send(0).start()
            for k in order[:1]:
                q_send(k).start()
            for n in range(min(2, len(own))):
                share.start(n)

        rows = pl.ds(pl.multiple_of(i * step_rows, step_rows), step_rows)
        fetch(i).wait()
        x = image[rows, :]
        k = dot(x, wkv_ref[0])
        k_ref[rows, :] = (k * head_scale(k, head_size)).astype(bf16)
        v = jnp.transpose(dot(x, wkv_ref[1])).astype(bf16)
        vt_ref[:, :head_size, rows] = v.reshape(width // head_size, head_size, step_rows)
        return carry

    lax.fori_loop(0, steps, project, 0)
    def forward(k, slot):
        block = queries.at[slot]
        return send(block, block, f_out.at[k], f_in.at[k], neighbour)

    def pair_send(k, s):
        return send(tiles.at[s], pair_tiles.at[k], p_out.at[k], p_in.at[k], neighbour)

    def far_send(k):
        return send(joined.at[k], far_tiles.at[k], c_out.at[k], c_in.at[k], peer(k))

    def turn_of(n):
        return min(len(turns) - 2, max(0, n - 3))

    def arrive(k):
        slot = lax.rem(line + k, lines) * 2 + side
        block = queries.at[slot]
        send(block, block, q_out.at[k], q_in.at[k], neighbour).wait_recv()
        forward(k, slot).start()

    def before(i):
        mine, k = turns[i]
        if not mine and k == lines:
            block = queries.at[line * 2 + 1 - side]
            send(block, block, q_out.at[0], q_in.at[0], neighbour).wait_recv()
        for j, later in enumerate(order):
            if j and i == max(0, 2 * j - 4):
                q_send(later).start()
        for taken in take.get(i, []):
            arrive(taken)
        if not mine and k < lines:
            forward(k, lax.rem(line + k, lines) * 2 + 1 - side).wait_recv()
        if own:
            for n in range(2, len(own)):
                if i == turn_of(n):
                    share.start(n)

    def after(i):
        mine, k = turns[i]
        if not mine and k < lines:
            pair_send(k, i).start()
        if i == min(1, len(turns) - 2):
            pair_send(lines, 0).start()
        for done in combine.get(i, []):
            pair_send(done, i).wait_recv()
            joined[done] = pack(
                *join([tiles[turns.index((True, done))], pair_tiles[done]], width)
            )
            far_send(done).start()
        if own:
            for n in range(len(own)):
                if i == min(len(turns) - 1, turn_of(n) + 1):
                    share.forward(n)

    def attend(s, carry):
        for i in range(len(turns)):
            pl.when(s == i)(functools.partial(before, i))
        k = pick(s, [k for _, k in turns])
        mine = pick(s, [int(m) for m, _ in turns])
        slot = lax.rem(line + k, lines) * 2 + mine * side + (1 - mine) * (1 - side)
        tiles[s] = attend_block(queries[slot], k_ref, vt_ref, head_size)
        for i in range(len(turns)):
            pl.when(s == i)(functools.partial(after, i))
        return carry

    lax.fori_loop(0, len(turns), attend, 0)
    pair_send(lines, 0).wait_recv()
    for k in range(1, lines):
        far_send(k).wait_recv()
    mixed, totals = join(
        [tiles[2 * lines - 1], pair_tiles[lines]] + [far_tiles[k] for k in range(1, lines)], width
    )
    for h in range(width // head_size):
        rows = slice(h * head_size, (h + 1) * head_size)
        mix = (mixed[rows] / totals[h : h + 1]).astype(bf16)
        for n in range(heads):
            out_ref[n, rows, :] = mix[:, n * rows_each : (n + 1) * rows_each]
    gather.drain()
    for k in range(lines):
        q_send(k).wait_send()
    for k in range(1, lines):
        forward(k, 0).wait_send()
        far_send(k).wait_send()
    for k in range(1, lines + 1):
        pair_send(k, 0).wait_send()
    for n in range(len(own)):
        share.finish(n)


def cross(tri, image, wq, wkv, weights, toks, heads, head_size, factor):
    rows, depth = tri.shape
    keys = image.shape[0]
    width = wq.shape[1]
    group = rows * heads
    lines = toks // 2
    tile = (width + 16, group)
    vmem = pl.BlockSpec(memory_space=pltpu.VMEM)
    anywhere = pl.BlockSpec(memory_space=pl.ANY)
    pieces = sum(w.shape[0] for w in weights)
    dma = pltpu.SemaphoreType.DMA
    return pl.pallas_call(
        functools.partial(
            cross_kernel, toks=toks, heads=heads, head_size=head_size, factor=factor,
            shared=len(weights),
        ),
        out_shape=[jax.ShapeDtypeStruct((heads, width, rows), bf16)]
        + [jax.ShapeDtypeStruct((heads,) + w.shape, bf16) for w in weights],
        in_specs=[vmem, anywhere, vmem, vmem] + [anywhere] * len(weights),
        out_specs=[vmem] + [anywhere] * len(weights),
        scratch_shapes=[
            pltpu.VMEM((keys, depth), bf16),
            pltpu.VMEM((keys, width), bf16),
            pltpu.VMEM((width // head_size, head_size + ONES, keys), bf16),
            pltpu.VMEM((toks, width, group), bf16),
            pltpu.VMEM((2 * lines,) + tile, bf16),
            pltpu.VMEM((lines + 1,) + tile, bf16),
            pltpu.VMEM((lines,) + tile, bf16),
            pltpu.VMEM((lines,) + tile, bf16),
            dma((keys // math.gcd(keys, STEP),)),
            dma((lines,)), dma((lines,)),
            dma((lines,)), dma((lines,)),
            dma((lines + 1,)), dma((lines + 1,)),
            dma((lines,)), dma((lines,)),
        ]
        + Gather.scratch(heads, rows, depth)
        + (Share.scratch(pieces, heads) if weights else []),
        compiler_params=pltpu.CompilerParams(
            vmem_limit_bytes=VMEM_LIMIT, collective_id=0, has_side_effects=True
        ),
        name="cross",
    )(tri, image, wq, wkv, *weights)


class Scatter:
    @staticmethod
    def scratch(heads, rows, depth):
        pairs = heads // 2
        dma = pltpu.SemaphoreType.DMA((pairs,))
        tiles = [pltpu.VMEM((pairs, rows, depth), bf16)] * 3
        return [pltpu.VMEM((pairs, 2, rows, depth), bf16)] + tiles + [dma] * 4

    def __init__(self, place, refs):
        self.place = place
        self.part, self.close, self.sums, self.distant = refs[:4]
        self.near_out, self.near_in, self.far_out, self.far_in = refs[4:]

    def near(self, k):
        p = self.place
        return send(
            self.part.at[k, 1 - p.core],
            self.close.at[k],
            self.near_out.at[k],
            self.near_in.at[k],
            p.partner(),
        )

    def far(self, k):
        return send(
            self.sums.at[k],
            self.distant.at[k],
            self.far_out.at[k],
            self.far_in.at[k],
            self.place.across(k),
        )

    def give(self, k, value):
        self.part[k] = value.reshape(self.part.shape[1:]).astype(bf16)
        self.near(k).start()

    def near_sum(self, k):
        self.near(k).wait_recv()
        return self.part[k, self.place.core].astype(f32) + self.close[k].astype(f32)

    def relay(self, k):
        self.sums[k] = self.near_sum(k).astype(bf16)
        self.far(k).start()

    def finish(self):
        total = self.near_sum(0)
        for k in range(1, self.place.pairs):
            self.far(k).wait_recv()
            total = total + self.distant[k].astype(f32)
        return total

    def drain(self):
        for k in range(self.place.pairs):
            self.near(k).wait_send()
        for k in range(1, self.place.pairs):
            self.far(k).wait_send()


def collect(place, scatter, mix, weight_ref):
    both = mix.shape[0] // place.pairs

    def partial(k):
        rows = pl.ds(pl.multiple_of(place.pair_at(k) * both, both), both)
        return dot(mix[rows, :], weight_ref[...])

    for k in range(1, place.pairs):
        scatter.give(k, partial(k))
    scatter.give(0, partial(0))
    for k in range(1, place.pairs):
        scatter.relay(k)
    return scatter.finish()


def self_kernel(
    tri_ref, mixed_ref, wout_ref, wqkv_ref, stream_ref, out_ref,
    mix, chunks, column, passed, k_ref, vt_ref, acc, results, landed,
    a_out, a_in, f_out, f_in, o_out, o_in, *refs,
    toks, heads, head_size, factor,
):
    place = Place(toks, heads)
    width, group = out_ref.shape
    count = width // head_size
    sharers = toks // count
    mine, part = lax.div(place.tok, sharers), lax.rem(place.tok, sharers)

    def owner(k):
        return lax.rem(mine + k + count, count)

    def owner_at(k):
        return (owner(k) * sharers + part, place.head)

    def sharer_at(m):
        return (mine * sharers + lax.rem(part + m, sharers), place.head)

    greet(
        place.head_peers()
        + [owner_at(k) for k in range(1, count)]
        + [sharer_at(m) for m in range(1, sharers)]
    )
    scatter = Scatter(place, refs[:8])
    gather = Gather(place, refs[8:])
    mix[...] = jnp.transpose(mixed_ref[...].astype(f32)).astype(bf16)
    vt_ref[head_size:, :] = jnp.ones((ONES, vt_ref.shape[1]), bf16)
    stream = tri_ref[...].astype(f32) + collect(place, scatter, mix, wout_ref)
    stream_ref[...] = stream
    gather.start(layer_norm(stream).astype(bf16))
    gather.forward()
    gather.finish()
    x = gather.rows[...].reshape(group, -1)
    for j in range(3):
        product = jnp.transpose(dot(x, wqkv_ref[j]))
        if j < 2:
            product = head_norm_rows(product, head_size, 1.0 if j else factor)
        chunks[:, j * head_size : (j + 1) * head_size, :] = product.reshape(
            count, head_size, group
        ).astype(bf16)

    def deal(k):
        return send(
            chunks.at[owner(k)], column.at[mine], a_out.at[k], a_in.at[k], owner_at(k)
        )

    def hand(k, m):
        source = column.at[owner(-k), pl.ds(head_size, 2 * head_size)]
        i = k * (sharers - 1) + m - 1
        return send(source, passed.at[k, m - 1], f_out.at[i], f_in.at[i], sharer_at(m))

    def fill(n, chunk):
        rows = slice(n * group, (n + 1) * group)
        k_ref[rows, :] = jnp.transpose(chunk[:head_size].astype(f32)).astype(bf16)
        vt_ref[:head_size, rows] = chunk[head_size:]

    for k in range(1, count):
        deal(k).start()
    column[mine] = chunks[mine]
    for k in range(count):
        if k:
            deal(k).wait_recv()
        for m in range(1, sharers):
            hand(k, m).start()
        fill(k, column[owner(-k), head_size:])

    def give_back(j):
        return send(results.at[j], landed.at[mine], o_out.at[j], o_in.at[j], owner_at(j + 1))

    span = count * group
    for m in range(sharers):
        if m:
            for k in range(count):
                hand(k, m).wait_recv()
                fill(m * count + k, passed[k, m - 1])
        keys = slice(m * span, (m + 1) * span)
        for j in range(count):
            scores = dot(k_ref[keys, :], column[owner(j + 1), :head_size])
            total = dot(vt_ref[:, keys], jnp.exp2(scores).astype(bf16))
            if m:
                total = acc[j] + total
            if m < sharers - 1:
                acc[j] = total
                continue
            result = (total[:head_size] / total[head_size : head_size + 1]).astype(bf16)
            if j == count - 1:
                landed[mine] = result
            else:
                results[j] = result
                give_back(j).start()
    for j in range(count - 1):
        give_back(j).wait_recv()
    out_ref[...] = landed[...].reshape(width, group)
    scatter.drain()
    gather.drain()
    for k in range(1, count):
        deal(k).wait_send()
    for k in range(count):
        for m in range(1, sharers):
            hand(k, m).wait_send()
    for j in range(count - 1):
        give_back(j).wait_send()


def self_stage(tri, mixed, wout, wqkv, toks, heads, head_size, factor):
    rows, depth = tri.shape
    width, group = mixed.shape
    count = width // head_size
    sharers = toks // count
    vmem = pl.BlockSpec(memory_space=pltpu.VMEM)
    dma = pltpu.SemaphoreType.DMA
    passes = max(1, count * (sharers - 1))
    return pl.pallas_call(
        functools.partial(
            self_kernel, toks=toks, heads=heads, head_size=head_size, factor=factor
        ),
        out_shape=[
            jax.ShapeDtypeStruct((rows, depth), f32),
            jax.ShapeDtypeStruct((width, group), bf16),
        ],
        in_specs=[vmem] * 4,
        out_specs=[vmem] * 2,
        scratch_shapes=[
            pltpu.VMEM((group, width), bf16),
            pltpu.VMEM((count, 3 * head_size, group), bf16),
            pltpu.VMEM((count, 3 * head_size, group), bf16),
            pltpu.VMEM((count, max(1, sharers - 1), 2 * head_size, group), bf16),
            pltpu.VMEM((toks * group, head_size), bf16),
            pltpu.VMEM((head_size + ONES, toks * group), bf16),
            pltpu.VMEM((count, head_size + ONES, group), f32),
            pltpu.VMEM((count, head_size, group), bf16),
            pltpu.VMEM((count, head_size, group), bf16),
            dma((count,)), dma((count,)),
            dma((passes,)), dma((passes,)),
            dma((count,)), dma((count,)),
        ] + Scatter.scratch(heads, rows, depth) + Gather.scratch(heads, rows, depth),
        compiler_params=pltpu.CompilerParams(
            vmem_limit_bytes=VMEM_LIMIT, collective_id=1, has_side_effects=True
        ),
        name="self_stage",
    )(tri, mixed, wout, wqkv)


def mlp_kernel(
    stream_ref, mixed_ref, wout_ref, win_ref, wdown_ref, out_ref, mix, *refs, toks, heads
):
    place = Place(toks, heads)
    greet(place.head_peers())
    scatter = Scatter(place, refs[:8])
    second = Scatter(place, refs[8:16])
    gather = Gather(place, refs[16:])
    mix[...] = jnp.transpose(mixed_ref[...].astype(f32)).astype(bf16)
    stream = stream_ref[...] + collect(place, scatter, mix, wout_ref)
    gather.start(layer_norm(stream).astype(bf16))

    def mlp(k):
        x = gather.rows[pl.ds(place.pair_at(k) * 2, 2)].reshape(-1, stream.shape[1])
        hidden = jax.nn.gelu(dot(x, win_ref[...]), approximate=True).astype(bf16)
        second.give(k, dot(hidden, wdown_ref[...]))

    gather.near_arrival(0).wait_recv()
    mlp(0)
    gather.forward()
    for k in range(1, place.pairs):
        gather.near_arrival(k).wait_recv()
    for k in range(1, place.pairs):
        mlp(k)
    for k in range(1, place.pairs):
        second.relay(k)
    out_ref[...] = (stream + second.finish()).astype(bf16)
    scatter.drain()
    second.drain()
    gather.drain()


def mlp_stage(stream, mixed, wout, win, wdown, toks, heads):
    rows, depth = stream.shape
    width, group = mixed.shape
    vmem = pl.BlockSpec(memory_space=pltpu.VMEM)
    return pl.pallas_call(
        functools.partial(mlp_kernel, toks=toks, heads=heads),
        out_shape=jax.ShapeDtypeStruct((rows, depth), bf16),
        in_specs=[vmem] * 5,
        out_specs=vmem,
        scratch_shapes=[pltpu.VMEM((group, width), bf16)]
        + Scatter.scratch(heads, rows, depth) * 2
        + Gather.scratch(heads, rows, depth),
        compiler_params=pltpu.CompilerParams(
            vmem_limit_bytes=VMEM_LIMIT, collective_id=2, has_side_effects=True
        ),
        name="mlp_stage",
    )(stream, mixed, wout, win, wdown)


def late_kernel(
    tri_ref, mixed_ref, cross_out_ref, qkv_ref, self_out_ref, win_ref, wdown_ref, out_ref,
    cross_out, qkv, self_out, win, down, mixes, chunks, column, passed, k_ref, vt_ref, acc,
    results, landed, load_sem, m_out, m_in, a_out, a_in, f_out, f_in, r_out, r_in, *refs,
    toks, heads, head_size, factor,
):
    place = Place(toks, heads)
    rows, depth = tri_ref.shape
    width = mixed_ref.shape[1]
    count = width // head_size
    sharers = toks // count
    sources = count * heads
    mine, part = lax.div(place.tok, sharers), lax.rem(place.tok, sharers)
    every = [(a, h) for h in range(heads) for a in range(count)]

    def owner(a):
        return lax.rem(mine + a + count, count)

    def column_at(h):
        return lax.rem(place.head + h + heads, heads)

    def device_at(a, h):
        return (owner(a) * sharers + part, column_at(h))

    def sharer_at(m):
        return (mine * sharers + lax.rem(part + m, sharers), place.head)

    def load(i):
        source, target = [
            (cross_out_ref, cross_out), (qkv_ref, qkv), (self_out_ref, self_out),
            (win_ref, win), (wdown_ref, down),
        ][i]
        return pltpu.make_async_copy(source, target, load_sem.at[i])

    for i in range(5):
        load(i).start()
    greet(
        [device_at(a, h) for a, h in every if (a, h) != (0, 0)]
        + [sharer_at(m) for m in range(1, sharers)]
    )
    scatter = Scatter(place, refs[:8])
    gather = Gather(place, refs[8:])

    def swap(h):
        return send(
            mixed_ref.at[column_at(h)], mixes.at[place.head], m_out.at[h], m_in.at[h],
            device_at(0, h),
        )

    for h in range(1, heads):
        swap(h).start()
    mixes[place.head] = mixed_ref[place.head]
    vt_ref[head_size:, :] = jnp.ones((ONES, vt_ref.shape[1]), bf16)
    load(0).wait()
    for h in range(1, heads):
        swap(h).wait_recv()

    def turned(ref):
        return jnp.transpose(ref[...].reshape(-1, rows).astype(f32)).astype(bf16)

    stream = tri_ref[...].astype(f32) + dot(turned(mixes), cross_out[...].reshape(-1, depth))
    x = layer_norm(stream).astype(bf16)
    load(1).wait()

    def deal(a, h):
        i = a * heads + h
        return send(
            chunks.at[column_at(h), owner(a)],
            column.at[mine * heads + place.head],
            a_out.at[i], a_in.at[i], device_at(a, h),
        )

    def project(h):
        n = column_at(h)
        for j in range(3):
            product = jnp.transpose(dot(x, qkv[n, j]))
            if j < 2:
                product = head_norm_rows(product, head_size, 1.0 if j else factor)
            chunks[n, :, j * head_size : (j + 1) * head_size, :] = product.reshape(
                count, head_size, rows
            ).astype(bf16)

    for h in range(heads):
        project(h)
        for a in sorted(range(count), key=lambda a: -min(a, count - a)):
            if (a, h) != (0, 0):
                deal(a, h).start()
    column[mine * heads + place.head] = chunks[place.head, mine]

    def slot_of(a, h):
        return owner(-a) * heads + column_at(-h)

    def hand(i, m):
        a, h = every[i]
        n = (m - 1) * sources + i
        source = column.at[slot_of(a, h), pl.ds(head_size, 2 * head_size)]
        return send(source, passed.at[m - 1, i], f_out.at[n], f_in.at[n], sharer_at(m))

    def fill(n, chunk):
        keys = slice(n * rows, (n + 1) * rows)
        k_ref[keys, :] = jnp.transpose(chunk[:head_size].astype(f32)).astype(bf16)
        vt_ref[:head_size, keys] = chunk[head_size:]

    for i, (a, h) in enumerate(every):
        if (a, h) != (0, 0):
            deal(a, h).wait_recv()
        for m in range(1, sharers):
            hand(i, m).start()
        fill(i, column[slot_of(a, h), head_size:])

    def give_back(a, h):
        i = a * heads + h
        return send(
            results.at[a, column_at(h)],
            landed.at[place.head * count + mine],
            r_out.at[i], r_in.at[i], device_at(a, h),
        )

    span = sources * rows
    blocks = [(j + 1) % count for j in range(count)]
    for m in range(sharers):
        if m:
            for i in range(sources):
                hand(i, m).wait_recv()
                fill(m * sources + i, passed[m - 1, i])
        keys = slice(m * span, (m + 1) * span)
        for a in blocks:
            queries = jnp.concatenate(
                [column[owner(a) * heads + n, :head_size] for n in range(heads)], axis=1
            )
            scores = dot(k_ref[keys, :], queries)
            total = dot(vt_ref[:, keys], jnp.exp2(scores).astype(bf16))
            if m:
                total = acc[a] + total
            if m < sharers - 1:
                acc[a] = total
                continue
            result = (total[:head_size] / total[head_size : head_size + 1]).astype(bf16)
            for n in range(heads):
                results[a, n] = result[:, n * rows : (n + 1) * rows]
            for h in range(heads):
                if (a, h) != (0, 0):
                    give_back(a, h).start()
    landed[place.head * count + mine] = results[0, place.head]
    for i in range(2, 5):
        load(i).wait()
    for a, h in every:
        if (a, h) != (0, 0):
            give_back(a, h).wait_recv()
    stream = stream + dot(turned(landed), self_out[...].reshape(-1, depth))
    gather.start(layer_norm(stream).astype(bf16))

    def mlp(k):
        x = gather.rows[pl.ds(place.pair_at(k) * 2, 2)].reshape(-1, depth)
        hidden = jax.nn.gelu(dot(x, win[...]), approximate=True).astype(bf16)
        scatter.give(k, dot(hidden, down[...]))

    gather.near_arrival(0).wait_recv()
    mlp(0)
    gather.forward()
    for k in range(1, place.pairs):
        gather.near_arrival(k).wait_recv()
    for k in range(1, place.pairs):
        for side in (1 - place.core, place.core):
            x = gather.rows[place.pair_at(k) * 2 + side]
            hidden = jax.nn.gelu(dot(x, win[...]), approximate=True).astype(bf16)
            scatter.part[k, side] = dot(hidden, down[...]).astype(bf16)
            if side is not place.core:
                scatter.near(k).start()
    for k in range(1, place.pairs):
        scatter.relay(k)
    out_ref[...] = (stream + scatter.finish()).astype(bf16)
    scatter.drain()
    gather.drain()
    for h in range(1, heads):
        swap(h).wait_send()
    for a, h in every:
        if (a, h) != (0, 0):
            deal(a, h).wait_send()
            give_back(a, h).wait_send()
    for i in range(sources):
        for m in range(1, sharers):
            hand(i, m).wait_send()


def late_stage(tri, mixed, cross_out, qkv, self_out, win, wdown, toks, heads, head_size, factor):
    rows, depth = tri.shape
    width = mixed.shape[1]
    count = width // head_size
    sharers = toks // count
    sources = count * heads
    vmem = pl.BlockSpec(memory_space=pltpu.VMEM)
    anywhere = pl.BlockSpec(memory_space=pl.ANY)
    dma = pltpu.SemaphoreType.DMA
    passes = max(1, sources * (sharers - 1))
    return pl.pallas_call(
        functools.partial(
            late_kernel, toks=toks, heads=heads, head_size=head_size, factor=factor
        ),
        out_shape=jax.ShapeDtypeStruct((rows, depth), bf16),
        in_specs=[vmem] * 2 + [anywhere] * 5,
        out_specs=vmem,
        scratch_shapes=[
            pltpu.VMEM(cross_out.shape, bf16),
            pltpu.VMEM(qkv.shape, bf16),
            pltpu.VMEM(self_out.shape, bf16),
            pltpu.VMEM(win.shape, bf16),
            pltpu.VMEM(wdown.shape, bf16),
            pltpu.VMEM((heads, width, rows), bf16),
            pltpu.VMEM((heads, count, 3 * head_size, rows), bf16),
            pltpu.VMEM((sources, 3 * head_size, rows), bf16),
            pltpu.VMEM((max(1, sharers - 1), sources, 2 * head_size, rows), bf16),
            pltpu.VMEM((toks * heads * rows, head_size), bf16),
            pltpu.VMEM((head_size + ONES, toks * heads * rows), bf16),
            pltpu.VMEM((count, head_size + ONES, heads * rows), f32),
            pltpu.VMEM((count, heads, head_size, rows), bf16),
            pltpu.VMEM((sources, head_size, rows), bf16),
            dma((5,)), dma((heads,)), dma((heads,)),
            dma((sources,)), dma((sources,)),
            dma((passes,)), dma((passes,)),
            dma((sources,)), dma((sources,)),
        ] + Scatter.scratch(heads, rows, depth) + Gather.scratch(heads, rows, depth),
        compiler_params=pltpu.CompilerParams(
            vmem_limit_bytes=VMEM_LIMIT, collective_id=3, has_side_effects=True
        ),
        name="late_stage",
    )(tri, mixed, cross_out, qkv, self_out, win, wdown)


def per_device(
    tri_tokens, image_tokens, cross_q, cross_kv, cross_out, self_qkv, self_out, mlp_in, mlp_out,
    *, tok, head
):
    rows, depth = tri_tokens.shape
    head_size = depth // HEADS
    factor = score_gain / math.sqrt(head_size) * math.log2(math.e)
    width = cross_q.shape[1]
    weights = []
    if rows % 128 == 0:
        weights = [
            cross_out.reshape(2, -1, depth),
            self_qkv.reshape(6, -1, width),
            self_out.reshape(2, -1, depth),
        ]
    mixed, *weights = cross(
        tri_tokens, image_tokens, cross_q, cross_kv, weights, tok, head, head_size, factor
    )
    if weights:
        weights[1] = weights[1].reshape(head, 3, depth, width)
        return late_stage(
            tri_tokens, mixed, *weights, mlp_in, mlp_out, tok, head, head_size, factor
        )
    mixed = mixed.transpose(1, 0, 2).reshape(mixed.shape[1], -1)
    stream, mixed = self_stage(
        tri_tokens, mixed, cross_out, self_qkv, tok, head, head_size, factor
    )
    return mlp_stage(stream, mixed, self_out, mlp_in, mlp_out, tok, head)


def solution(mesh):
    return jax.shard_map(
        functools.partial(per_device, tok=mesh.shape["tok"], head=mesh.shape["head"]),
        mesh=mesh,
        in_specs=(
            P(("tok", "head"), None),
            P("tok", None),
            P(None, "head"),
            P(None, None, "head"),
            P("head", None),
            P(None, None, "head"),
            P("head", None),
            P(None, "head"),
            P("head", None),
        ),
        out_specs=P(("tok", "head"), None),
        check_vma=False,
    )
```
